128 devices in a mesh: row: 8 (over x_hi, y), col: 16 (over z, x_lo, core).
Axes of the slice: x: 4 (x_hi: 2, x_lo: 2; x = x_hi * 2 + x_lo), y: 4, z: 4, core: 2. Of those that a mesh axis runs over, the one named last changes fastest.
Arguments:
- latent: bfloat16 [16, 524288], P(None, ('row', 'col')), may hold values from -200 to 200, as said below
- in_weight: bfloat16 [3, 3, 16, 512], replicated, may hold values from -0.5 to 0.5
- in_bias: float32 [512], replicated, may hold values from -3 to 3
- norm_gain: float32 [512], replicated, may hold values from 0.25 to 1.75
- norm_shift: float32 [512], replicated, may hold values from -3 to 3
- mid_weight: bfloat16 [512, 3, 3, 512], replicated, may hold values from -0.09375 to 0.09375
- mid_bias: float32 [512], replicated, may hold values from -3 to 3
Outputs:
- features: bfloat16 [512, 1024, 512], P('row', 'col')
The draws below stay inside these ranges and needn't reach their ends.
Inputs may be any that keep to these rules, and one draw needn't show every extreme that they name: real-valued latent entries.
All inputs are finite; a program needn't handle non-finite values.
Results may differ from the reference program's by a relative error of at most 0.0095.
Values may be sent and summed in bfloat16 or wider, within the bound.
No kernel may reach another device: no remote copies, remote signals or barrier semaphores. Data moves between devices by JAX's collectives and lax.ppermute only.
A program may use at most 192 MiB of HBM per device.

```python
import jax
import jax.numpy as jnp
from jax import lax

C_LAT = 16
CH = 512
GROUPS = 32
TILE_H = 64
TILE_W = 64
N_ROW = 8
N_COL = 16


def draw_latent(key, part):
    first_key, second_key, third_key = jax.random.split(jax.random.fold_in(key, 11), 3)
    height = TILE_H * N_ROW
    breadth = TILE_W * N_COL
    ramp = jnp.arange(height, dtype=jnp.float32) / (height - 1)
    values = jnp.clip(jax.random.normal(first_key, (C_LAT, height, breadth), jnp.float32), -4.0, 4.0)
    values = values + (0.5 + ramp)[None, :, None]
    row_scale = jnp.exp(ramp * 1.0986) * jax.random.uniform(second_key, (height,), jnp.float32, 0.7, 1.3)
    col_scale = jax.random.uniform(third_key, (breadth,), jnp.float32, 0.7, 1.3)
    field = values * row_scale[None, :, None] * col_scale[None, None, :]
    return field.reshape(C_LAT, height * breadth).astype(jnp.bfloat16)


def gaussian(stream_key, shape, spread, reach, kind=jnp.bfloat16):
    result = spread * jax.random.normal(stream_key, shape, jnp.float32)
    return jnp.clip(result, min=-reach, max=reach).astype(kind)


def setup_inputs(seed: int = 0) -> dict:
    keys = jax.random.split(jax.random.key(seed), 8)
    latent = draw_latent(jax.random.fold_in(keys[7], 71), 0)
    in_weight = gaussian(keys[1], (3, 3, C_LAT, CH), (9 * C_LAT) ** -0.5, 0.5)
    in_bias = gaussian(keys[2], (CH,), 0.5, 3.0, jnp.float32)
    norm_gain = jnp.clip(1.0 + 0.15 * jax.random.normal(keys[3], (CH,), jnp.float32), 0.25, 1.75)
    norm_shift = gaussian(keys[4], (CH,), 0.5, 3.0, jnp.float32)
    mid_weight = gaussian(keys[5], (CH, 3, 3, CH), (9 * CH) ** -0.5, 0.09375)
    mid_bias = gaussian(keys[6], (CH,), 0.5, 3.0, jnp.float32)
    return {"latent": latent, "in_weight": in_weight, "in_bias": in_bias, "norm_gain": norm_gain, "norm_shift": norm_shift, "mid_weight": mid_weight, "mid_bias": mid_bias}


EPSILON = 1e-06

def reference(latent, in_weight, in_bias, norm_gain, norm_shift, mid_weight, mid_bias):
    height = TILE_H * N_ROW
    breadth = TILE_W * N_COL
    picture = latent.reshape(1, C_LAT, height, breadth)
    first_out = lax.conv_general_dilated(picture, in_weight, (1, 1), ((1, 1), (1, 1)), dimension_numbers=('NCHW', 'HWIO', 'NHWC'), preferred_element_type=jnp.float32)[0]
    first_out = (first_out + in_bias).astype(jnp.bfloat16)
    grouped = first_out.astype(jnp.float32).reshape(height * breadth, GROUPS, CH // GROUPS)
    cells = height * breadth * (CH // GROUPS)
    group_mean = lax.optimization_barrier(jnp.sum(grouped, axis=(0, 2))) / cells
    centred = grouped - group_mean[None, :, None]
    group_var = lax.optimization_barrier(jnp.sum(centred * centred, axis=(0, 2))) / cells
    normed = centred * lax.rsqrt(group_var + EPSILON)[None, :, None]
    normed = normed.reshape(height, breadth, CH) * norm_gain + norm_shift
    activated = jax.nn.silu(normed).astype(jnp.bfloat16)
    features = lax.conv_general_dilated(activated[None], mid_weight, (1, 1), ((1, 1), (1, 1)), dimension_numbers=('NHWC', 'OHWI', 'NHWC'), preferred_element_type=jnp.float32)[0]
    return (features + mid_bias).astype(jnp.bfloat16)
```

```python
import functools

import jax
import jax.numpy as jnp
from jax import lax
from jax.experimental import pallas as pl
from jax.experimental.pallas import tpu as pltpu
from jax.sharding import PartitionSpec as P

C_LAT = 16
CH = 512
GROUPS = 32
TILE = 64
WIDTH = 1024
N_ROW = 8
N_COL = 16
N_DEV = N_ROW * N_COL
OWN = 4
ACT = TILE + 2
LAT = TILE + 4
PLANES = 6
EPSILON = 1e-06
BF16 = jnp.bfloat16
F32 = jnp.float32
VMEM = pl.BlockSpec(memory_space=pltpu.VMEM)
SMEM = pl.BlockSpec(memory_space=pltpu.SMEM)
MIB = 1 << 20


def dot_tn(lhs, rhs):
    return lax.dot_general(lhs, rhs, (((0,), (0,)), ((), ())), preferred_element_type=F32)


def dot_nt(lhs, rhs):
    return lax.dot_general(lhs, rhs, (((1,), (1,)), ((), ())), preferred_element_type=F32)


def pack_kernel(own, top, bot, out, rows):
    rows[0:16] = top[:, 0:WIDTH]
    rows[16:32] = top[:, WIDTH:]
    for r in range(OWN):
        rows[32 + 16 * r : 48 + 16 * r] = own[:, WIDTH * r : WIDTH * (r + 1)]
    rows[96:112] = bot[:, 0:WIDTH]
    rows[112:128] = bot[:, WIDTH:]
    k = lax.broadcasted_iota(jnp.int32, (384, 256), 0)
    n = lax.broadcasted_iota(jnp.int32, (384, 256), 1)
    lane = n % 128
    column = 64 * (n // 128) + 4 * (lane % 16) + lane // 16 + 126
    pick = jnp.where(k == column, 1.0, 0.0).astype(BF16)
    zero = jnp.zeros((128, 128), BF16)
    for t in range(8):
        parts = [
            rows[:, 128 * u : 128 * (u + 1)] if 0 <= u < 8 else zero for u in (t - 1, t, t + 1)
        ]
        moved = jnp.dot(jnp.concatenate(parts, axis=1), pick, preferred_element_type=F32)
        out[2 * t] = moved[:, :128].astype(BF16)
        out[2 * t + 1] = moved[:, 128:].astype(BF16)


def stats_kernel(own, top, bot, weight, bias, out, taps):
    column = lax.broadcasted_iota(jnp.int32, (C_LAT, WIDTH), 1)
    for r in range(OWN + 2):
        if r == 0:
            row = top[:, WIDTH:]
        elif r == OWN + 1:
            row = bot[:, 0:WIDTH]
        else:
            row = own[:, WIDTH * (r - 1) : WIDTH * r]
        wide = row.astype(F32)
        left = jnp.where(column == 0, 0.0, pltpu.roll(wide, 1, 1))
        right = jnp.where(column == WIDTH - 1, 0.0, pltpu.roll(wide, WIDTH - 1, 1))
        at = slice(16 * r, 16 * r + 16)
        taps[0, at] = left.astype(BF16)
        taps[1, at] = row
        taps[2, at] = right.astype(BF16)
    total = jnp.zeros((8, CH), F32)
    squares = jnp.zeros((8, CH), F32)
    for r in range(OWN):
        for half in range(2):
            cols = slice(512 * half, 512 * half + 512)
            patch = jnp.concatenate([taps[b, 16 * r : 16 * r + 48, cols] for b in range(3)], axis=0)
            value = (dot_tn(patch, weight[...]) + bias[...]).reshape(64, 8, CH)
            total = total + jnp.sum(value, axis=0)
            squares = squares + jnp.sum(value * value, axis=0)
    channel = lax.broadcasted_iota(jnp.int32, (CH, 128), 0) // (CH // GROUPS)
    lane = lax.broadcasted_iota(jnp.int32, (CH, 128), 1)
    to_sum = jnp.where(channel == lane, 1.0, 0.0)
    to_squares = jnp.where(channel == lane - GROUPS, 1.0, 0.0)
    both = jnp.dot(
        total, to_sum, precision=lax.Precision.HIGHEST, preferred_element_type=F32
    ) + jnp.dot(squares, to_squares, precision=lax.Precision.HIGHEST, preferred_element_type=F32)
    out[...] = jnp.broadcast_to(jnp.sum(both, axis=0).reshape(1, 1, 128), (N_DEV, 1, 128))


def affine(stats, bias, gain, shift):
    sums = jnp.sum(stats[...], axis=0)
    sums = jnp.broadcast_to(sums, (8, 128)) / (TILE * TILE * N_DEV * (CH // GROUPS))
    channel = lax.broadcasted_iota(jnp.int32, (128, CH), 1) // (CH // GROUPS)
    lane = lax.broadcasted_iota(jnp.int32, (128, CH), 0)
    spread = functools.partial(
        jnp.dot, precision=lax.Precision.HIGHEST, preferred_element_type=F32
    )
    mean = spread(sums, jnp.where(channel == lane, 1.0, 0.0))[0:1]
    square = spread(sums, jnp.where(channel == lane - GROUPS, 1.0, 0.0))[0:1]
    scale = lax.rsqrt(square - mean * mean + EPSILON) * gain[...]
    return scale, (bias[...] - mean) * scale + shift[...]


def main_kernel(
    place, recv, stats, in_weight, in_bias, gain, shift, weight, bias, out, lat, act, spread
):
    for s in range(N_COL):
        first, last = (0 if s == 0 else 32), (128 if s == N_COL - 1 else 96)
        rows = recv[s, first:last]
        wide = rows.astype(F32)
        at = pl.ds(64 * s + first, last - first)
        lat[0, at] = rows
        for b in (1, 2):
            lat[b, at] = pltpu.roll(wide, 128 - 16 * b, 1).astype(BF16)
    scale, offset = affine(stats, in_bias, gain, shift)
    half_scale, half_offset = 0.5 * scale, 0.5 * offset
    batch = 6

    def activate(step, _):
        row = step * batch
        patches = [
            jnp.concatenate(
                [lat[b, pl.ds(pl.multiple_of((row + j) * 16, 16), 48)] for b in range(3)], axis=0
            )
            for j in range(batch)
        ]
        value = dot_tn(jnp.concatenate(patches, axis=1), in_weight[...])
        for j in range(batch):
            half = value[128 * j : 128 * j + 96] * half_scale + half_offset
            act[row + j] = (half + half * jnp.tanh(half)).astype(BF16)
        return 0

    lax.fori_loop(0, ACT // batch, activate, 0)

    @pl.when(place[0] == 0)
    def _():
        act[0] = jnp.zeros((PLANES * 16, CH), BF16)

    @pl.when(place[0] == N_ROW - 1)
    def _():
        act[ACT - 1] = jnp.zeros((PLANES * 16, CH), BF16)

    cell = lax.broadcasted_iota(jnp.int32, (ACT, 16, CH), 1)

    @pl.when(place[1] == 0)
    def _():
        act[:, 0:16] = jnp.where(cell == 0, 0.0, act[:, 0:16].astype(F32)).astype(BF16)

    @pl.when(place[1] == N_COL - 1)
    def _():
        act[:, 80:96] = jnp.where(cell == 15, 0.0, act[:, 80:96].astype(F32)).astype(BF16)

    deep = 16

    def convolve(step, _):
        row = step * deep
        total = jnp.broadcast_to(bias[...], (deep * TILE, CH))
        for a in range(3):
            for b in range(3):
                cells = act[pl.ds(row + a, deep), 16 * b : 16 * b + 64].reshape(deep * TILE, CH)
                total = total + dot_nt(cells, weight[a, b])
        for r in range(deep):
            for t in range(4):
                at = 64 * r + 16 * t
                for l in range(4):
                    lanes = slice(128 * l, 128 * l + 128)
                    spread[r, l, pl.ds(t, 16, stride=4)] = total[at : at + 16, lanes]
        for r in range(deep):
            for l in range(4):
                out[row + r, :, 128 * l : 128 * l + 128] = spread[r, l].astype(BF16)
        return 0

    lax.fori_loop(0, TILE // deep, convolve, 0)


def body(latent, in_weight, in_bias, norm_gain, norm_shift, mid_weight, mid_bias):
    both = ("row", "col")
    up = [(i, i + 1) for i in range(N_DEV - 1)]
    down = [(i + 1, i) for i in range(N_DEV - 1)]
    top = lax.ppermute(latent[:, 2 * WIDTH :], both, up)
    bot = lax.ppermute(latent[:, : 2 * WIDTH], both, down)
    chunks = pl.pallas_call(
        pack_kernel,
        out_shape=jax.ShapeDtypeStruct((N_COL, 128, 128), BF16),
        in_specs=[VMEM] * 3,
        out_specs=VMEM,
        scratch_shapes=[pltpu.VMEM((128, WIDTH), BF16)],
        name="pack",
    )(latent, top, bot)
    recv = lax.all_to_all(chunks, "col", split_axis=0, concat_axis=0, tiled=True)
    taps = jnp.transpose(in_weight, (1, 0, 2, 3)).reshape(9 * C_LAT, CH)
    bias = in_bias.reshape(1, CH)
    partial = pl.pallas_call(
        stats_kernel,
        out_shape=jax.ShapeDtypeStruct((N_DEV, 1, 128), F32),
        in_specs=[VMEM] * 5,
        out_specs=VMEM,
        scratch_shapes=[pltpu.VMEM((3, 96, WIDTH), BF16)],
        name="stats",
    )(latent, top, bot, taps, bias)
    stats = lax.all_to_all(partial, both, split_axis=0, concat_axis=0, tiled=True)
    place = jnp.stack([lax.axis_index("row"), lax.axis_index("col")]).astype(jnp.int32)
    return pl.pallas_call(
        main_kernel,
        out_shape=jax.ShapeDtypeStruct((TILE, TILE, CH), BF16),
        in_specs=[SMEM] + [VMEM] * 8,
        out_specs=VMEM,
        scratch_shapes=[
            pltpu.VMEM((3, LAT * 16, 128), BF16),
            pltpu.VMEM((ACT, PLANES * 16, CH), BF16),
            pltpu.VMEM((16, 4, TILE, 128), F32),
        ],
        compiler_params=pltpu.CompilerParams(vmem_limit_bytes=48 * MIB),
        name="main",
    )(
        place,
        recv,
        stats,
        taps,
        bias,
        norm_gain.reshape(1, CH),
        norm_shift.reshape(1, CH),
        jnp.transpose(mid_weight, (1, 2, 0, 3)),
        mid_bias.reshape(1, CH),
    )


def solution(mesh):
    in_specs = (P(None, ("row", "col")), P(), P(), P(), P(), P(), P())
    return jax.shard_map(
        body, mesh=mesh, in_specs=in_specs, out_specs=P("row", "col", None), check_vma=False
    )
```

```python
import functools

import jax
import jax.numpy as jnp
from jax import lax
from jax.experimental import pallas as pl
from jax.experimental.pallas import tpu as pltpu
from jax.sharding import PartitionSpec as P

C_LAT = 16
CH = 512
GROUPS = 32
TILE = 64
WIDTH = 1024
N_ROW = 8
N_COL = 16
N_DEV = N_ROW * N_COL
OWN = 4
ACT = TILE + 2
LAT = TILE + 4
PLANES = 6
EPSILON = 1e-06
BF16 = jnp.bfloat16
F32 = jnp.float32
VMEM = pl.BlockSpec(memory_space=pltpu.VMEM)
SMEM = pl.BlockSpec(memory_space=pltpu.SMEM)
HBM = pl.BlockSpec(memory_space=pltpu.HBM)
MIB = 1 << 20


def dot_tn(lhs, rhs):
    return lax.dot_general(lhs, rhs, (((0,), (0,)), ((), ())), preferred_element_type=F32)


def dot_nt(lhs, rhs):
    return lax.dot_general(lhs, rhs, (((1,), (1,)), ((), ())), preferred_element_type=F32)


def hbm(array):
    return pltpu.with_memory_space_constraint(array, pltpu.HBM)


def start_copies(sources, targets, sems):
    copies = [
        pltpu.make_async_copy(source, target, sems.at[i])
        for i, (source, target) in enumerate(zip(sources, targets))
    ]
    for copy in copies:
        copy.start()
    return copies


def pack_kernel(place, own_hbm, top, bot, out, rows, own, sems):
    copies = start_copies((own_hbm,), (own,), sems)

    @pl.when(place[1] == 0)
    def _():
        rows[64:80] = top[:, 0:WIDTH]
        rows[80:96] = top[:, WIDTH:]

    @pl.when(place[1] != 0)
    def _():
        rows[64:80] = bot[:, 0:WIDTH]
        rows[80:96] = bot[:, WIDTH:]

    k = lax.broadcasted_iota(jnp.int32, (384, 256), 0)
    n = lax.broadcasted_iota(jnp.int32, (384, 256), 1)
    lane = n % 128
    column = 64 * (n // 128) + 4 * (lane % 16) + lane // 16 + 126
    pick = jnp.where(k == column, 1.0, 0.0).astype(BF16)
    zero = jnp.zeros((96, 128), BF16)
    copies[0].wait()
    for r in range(OWN):
        rows[16 * r : 16 * r + 16] = own[:, WIDTH * r : WIDTH * (r + 1)]
    for t in range(8):
        parts = [
            rows[:, 128 * u : 128 * (u + 1)] if 0 <= u < 8 else zero for u in (t - 1, t, t + 1)
        ]
        moved = jnp.dot(jnp.concatenate(parts, axis=1), pick, preferred_element_type=F32)
        out[2 * t] = moved[:, :128].astype(BF16)
        out[2 * t + 1] = moved[:, 128:].astype(BF16)


def stats_kernel(own_hbm, top, bot, weight_hbm, bias_hbm, out, taps, own, weight, bias, sems):
    copies = start_copies((own_hbm, weight_hbm, bias_hbm), (own, weight, bias), sems)
    copies[0].wait()
    column = lax.broadcasted_iota(jnp.int32, (C_LAT, WIDTH), 1)
    for r in range(OWN + 2):
        if r == 0:
            row = top[:, WIDTH:]
        elif r == OWN + 1:
            row = bot[:, 0:WIDTH]
        else:
            row = own[:, WIDTH * (r - 1) : WIDTH * r]
        wide = row.astype(F32)
        left = jnp.where(column == 0, 0.0, pltpu.roll(wide, 1, 1))
        right = jnp.where(column == WIDTH - 1, 0.0, pltpu.roll(wide, WIDTH - 1, 1))
        at = slice(16 * r, 16 * r + 16)
        taps[0, at] = left.astype(BF16)
        taps[1, at] = row
        taps[2, at] = right.astype(BF16)
    copies[1].wait()
    copies[2].wait()
    total = jnp.zeros((8, CH), F32)
    squares = jnp.zeros((8, CH), F32)
    for r in range(OWN):
        for half in range(2):
            cols = slice(512 * half, 512 * half + 512)
            patch = jnp.concatenate(
                [taps[b, 16 * (r + a) : 16 * (r + a) + 16, cols] for a in range(3) for b in range(3)],
                axis=0,
            )
            value = (dot_tn(patch, weight[...]) + bias[...]).reshape(64, 8, CH)
            total = total + jnp.sum(value, axis=0)
            squares = squares + jnp.sum(value * value, axis=0)
    channel = lax.broadcasted_iota(jnp.int32, (CH, 128), 0) // (CH // GROUPS)
    lane = lax.broadcasted_iota(jnp.int32, (CH, 128), 1)
    to_sum = jnp.where(channel == lane, 1.0, 0.0)
    to_squares = jnp.where(channel == lane - GROUPS, 1.0, 0.0)
    both = jnp.dot(
        total, to_sum, precision=lax.Precision.HIGHEST, preferred_element_type=F32
    ) + jnp.dot(squares, to_squares, precision=lax.Precision.HIGHEST, preferred_element_type=F32)
    out[...] = jnp.broadcast_to(jnp.sum(both, axis=0).reshape(1, 1, 128), (N_DEV, 1, 128))


def affine(stats, bias, gain, shift):
    sums = jnp.sum(stats[...], axis=0)
    sums = jnp.broadcast_to(sums, (8, 128)) / (TILE * TILE * N_DEV * (CH // GROUPS))
    channel = lax.broadcasted_iota(jnp.int32, (128, CH), 1) // (CH // GROUPS)
    lane = lax.broadcasted_iota(jnp.int32, (128, CH), 0)
    spread = functools.partial(
        jnp.dot, precision=lax.Precision.HIGHEST, preferred_element_type=F32
    )
    mean = spread(sums, jnp.where(channel == lane, 1.0, 0.0))[0:1]
    square = spread(sums, jnp.where(channel == lane - GROUPS, 1.0, 0.0))[0:1]
    scale = lax.rsqrt(square - mean * mean + EPSILON) * gain[...]
    return scale, (bias[...] - mean) * scale + shift[...]


def prepare_kernel(weight, points):
    def thirds(g):
        even = 0.5 * (g[0] + g[2])
        odd = 0.5 * g[1]
        return g[0], even + odd, even - odd, g[2]

    def transform(step, _):
        rows = pl.ds(pl.multiple_of(step * 16, 16), 16)
        for l in range(4):
            lanes = slice(128 * l, 128 * l + 128)
            columns = [
                thirds([weight[a, b, rows, lanes].astype(F32) for a in range(3)]) for b in range(3)
            ]
            for u in range(4):
                for v, value in enumerate(thirds([columns[b][u] for b in range(3)])):
                    points[4 * u + v, rows, lanes] = value.astype(BF16)
        return 0

    lax.fori_loop(0, weight.shape[2] // 16, transform, 0)


BLOCK = 8
N_BLOCK = TILE // 2 // BLOCK
M_ROWS = BLOCK * 32


def main_kernel(
    place,
    recv,
    stats,
    taps_hbm,
    bias_hbm,
    gain_hbm,
    shift_hbm,
    mid_bias_hbm,
    points_hbm,
    out_hbm,
    lat,
    act,
    affines,
    v0,
    v1,
    m0,
    m1,
    spread,
    out,
    taps,
    vectors,
    points,
    in_sems,
    sems,
):
    loads = start_copies(
        (taps_hbm, bias_hbm, gain_hbm, shift_hbm, mid_bias_hbm, points_hbm),
        (taps, *(vectors.at[i : i + 1] for i in range(4)), points),
        in_sems,
    )
    v_slots, m_slots = (v0, v1), (m0, m1)
    for s in range(N_COL):
        rows = recv[s].astype(F32)
        moved = [rows] + [pltpu.roll(rows, 128 - 16 * b, 1) for b in (1, 2)]
        for b in range(3):
            value = moved[b].astype(BF16)
            lat[b, 32 + 64 * s : 96 + 64 * s] = value[0:64]
            if s == 0:
                lat[b, 0:32] = value[64:96]
            if s == N_COL - 1:
                lat[b, 32 + 64 * N_COL :] = value[64:96]
    for load in loads[:-1]:
        load.wait()
    scale, offset = affine(stats, vectors[0:1], vectors[1:2], vectors[2:3])
    cell = lax.broadcasted_iota(jnp.int32, (16, CH), 0)
    hide_low = jnp.logical_and(cell == 0, place[1] == 0)
    hide_high = jnp.logical_and(cell == 15, place[1] == N_COL - 1)
    for i, value in enumerate((0.5 * scale, 0.5 * offset)):
        wide = jnp.broadcast_to(value, (16, CH))
        affines[i, 0] = jnp.where(hide_low, 0.0, wide)
        affines[i, 1] = wide
        affines[i, 2] = jnp.where(hide_high, 0.0, wide)

    def activate(pair):
        patches = []
        for j in range(2):
            at = pl.multiple_of((2 * pair + j) * 16, 16)
            patches.append(
                jnp.concatenate(
                    [lat[b, pl.ds(at + 16 * a, 16)] for a in range(3) for b in range(3)], axis=0
                )
            )
        value = dot_tn(jnp.concatenate(patches, axis=1), taps[...])
        for j in range(2):
            row = 2 * pair + j
            hidden = jnp.logical_or(
                jnp.logical_and(row == 0, place[0] == 0),
                jnp.logical_and(row == ACT - 1, place[0] == N_ROW - 1),
            )
            keep = jnp.where(hidden, 0.0, 1.0)
            for t in range(PLANES):
                kind = 0 if t == 0 else (2 if t == PLANES - 1 else 1)
                at = 128 * j + 16 * t
                half = value[at : at + 16] * (affines[0, kind] * keep) + affines[1, kind] * keep
                act[row, 16 * t : 16 * t + 16] = (half + half * jnp.tanh(half)).astype(BF16)

    def build(tile, slot):
        base = pl.multiple_of((tile % BLOCK) * 32, 32)
        for l in range(4):
            lanes = slice(128 * l, 128 * l + 128)
            rows = []
            for t in range(PLANES):
                d = [act[2 * tile + u, 16 * t : 16 * t + 16, lanes] for u in range(4)]
                rows.append((d[0] - d[2], d[1] + d[2], d[2] - d[1], d[1] - d[3]))
            for u in range(4):
                for q in range(2):
                    r = [rows[2 * q + v][u] for v in range(4)]
                    columns = (r[0] - r[2], r[1] + r[2], r[2] - r[1], r[1] - r[3])
                    for v in range(4):
                        slot[4 * u + v, pl.ds(base + 16 * q, 16), lanes] = columns[v]

    def multiply(point, v_slot, m_slot):
        m_slot[point] = dot_nt(v_slot[point], points[point])

    def finish(tile, slot):
        base = pl.multiple_of((tile % BLOCK) * 32, 32)
        for l in range(4):
            lanes = slice(128 * l, 128 * l + 128)
            bias = vectors[3:4, lanes]
            for q in range(2):
                sums = []
                for u in range(4):
                    m = [slot[4 * u + v, pl.ds(base + 16 * q, 16), lanes] for v in range(4)]
                    both, apart = m[1] + m[2], m[1] - m[2]
                    sums.append((m[0] + both, apart - m[3]))
                for f in range(2):
                    z = [sums[u][f] for u in range(4)]
                    both, apart = z[1] + z[2], z[1] - z[2]
                    spread[0, l, pl.ds(2 * q + f, 16, stride=4)] = z[0] + both + bias
                    spread[1, l, pl.ds(2 * q + f, 16, stride=4)] = apart - z[3] + bias
            for e in range(2):
                out[2 * tile + e, :, lanes] = spread[e, l].astype(BF16)

    activate(0)
    activate(1)

    def warm(c, _):
        build(c, v0)
        activate(c + 2)
        return 0

    lax.fori_loop(0, BLOCK, warm, 0)
    loads[-1].wait()
    last_pair = ACT // 2 - 1
    copies = []
    for n in range(N_BLOCK):
        this_v, next_v = v_slots[n % 2], v_slots[1 - n % 2]
        this_m, last_m = m_slots[n % 2], m_slots[1 - n % 2]

        def steady(c, _, n=n, this_v=this_v, next_v=next_v, this_m=this_m, last_m=last_m):
            g = n * BLOCK + c
            multiply(2 * c, this_v, this_m)
            if n > 0:
                finish(g - BLOCK, last_m)
            multiply(2 * c + 1, this_v, this_m)
            if n < N_BLOCK - 1:
                build(g + BLOCK, next_v)
                activate(jnp.minimum(g + BLOCK + 2, last_pair))
            return 0

        lax.fori_loop(0, BLOCK, steady, 0)
        if n > 0:
            copies.append(send(out, out_hbm, n - 1, sems))

    def drain(c, _):
        finish((N_BLOCK - 1) * BLOCK + c, m_slots[1 - N_BLOCK % 2])
        return 0

    lax.fori_loop(0, BLOCK, drain, 0)
    copies.append(send(out, out_hbm, N_BLOCK - 1, sems))
    for copy in copies:
        copy.wait()


def send(out, out_hbm, n, sems):
    rows = slice(2 * BLOCK * n, 2 * BLOCK * (n + 1))
    copy = pltpu.make_async_copy(out.at[rows], out_hbm.at[rows], sems.at[n])
    copy.start()
    return copy


def step(latent, in_weight, in_bias, norm_gain, norm_shift, mid_weight, mid_bias):
    both = ("row", "col")
    up = [(i, i + 1) for i in range(N_DEV - 1)]
    down = [(i + 1, i) for i in range(N_DEV - 1)]
    top = lax.ppermute(latent[:, 2 * WIDTH :], both, up)
    bot = lax.ppermute(latent[:, : 2 * WIDTH], both, down)
    taps = in_weight.reshape(9 * C_LAT, CH)
    bias = in_bias.reshape(1, CH)
    place = jnp.stack([lax.axis_index("row"), lax.axis_index("col")]).astype(jnp.int32)
    chunks = pl.pallas_call(
        pack_kernel,
        out_shape=jax.ShapeDtypeStruct((N_COL, 96, 128), BF16),
        in_specs=[SMEM, HBM, VMEM, VMEM],
        out_specs=VMEM,
        scratch_shapes=[
            pltpu.VMEM((96, WIDTH), BF16),
            pltpu.VMEM((C_LAT, OWN * WIDTH), BF16),
            pltpu.SemaphoreType.DMA((1,)),
        ],
        compiler_params=pltpu.CompilerParams(vmem_limit_bytes=8 * MIB),
        name="pack",
    )(place, hbm(latent), top, bot)
    recv = lax.all_to_all(chunks, "col", split_axis=0, concat_axis=0, tiled=True)
    partial = pl.pallas_call(
        stats_kernel,
        out_shape=jax.ShapeDtypeStruct((N_DEV, 1, 128), F32),
        in_specs=[HBM, VMEM, VMEM, HBM, HBM],
        out_specs=VMEM,
        scratch_shapes=[
            pltpu.VMEM((3, 96, WIDTH), BF16),
            pltpu.VMEM((C_LAT, OWN * WIDTH), BF16),
            pltpu.VMEM((9 * C_LAT, CH), BF16),
            pltpu.VMEM((1, CH), F32),
            pltpu.SemaphoreType.DMA((3,)),
        ],
        compiler_params=pltpu.CompilerParams(vmem_limit_bytes=12 * MIB),
        name="stats",
    )(hbm(latent), top, bot, hbm(taps), hbm(bias))
    stats = lax.all_to_all(partial, both, split_axis=0, concat_axis=0, tiled=True)
    points = pl.pallas_call(
        prepare_kernel,
        out_shape=jax.ShapeDtypeStruct((16, CH, CH), BF16),
        grid=(8,),
        in_specs=[pl.BlockSpec((3, 3, CH // 8, CH), lambda i: (0, 0, i, 0))],
        out_specs=pl.BlockSpec((16, CH // 8, CH), lambda i: (0, i, 0)),
        compiler_params=pltpu.CompilerParams(vmem_limit_bytes=60 * MIB),
        name="prepare",
    )(hbm(jnp.transpose(mid_weight, (1, 2, 0, 3))))
    return pl.pallas_call(
        main_kernel,
        out_shape=jax.ShapeDtypeStruct((TILE, TILE, CH), BF16),
        in_specs=[SMEM, VMEM, VMEM] + [HBM] * 6,
        out_specs=HBM,
        scratch_shapes=[
            pltpu.VMEM((3, LAT * 16, 128), BF16),
            pltpu.VMEM((ACT, PLANES * 16, CH), BF16),
            pltpu.VMEM((2, 3, 16, CH), F32),
            pltpu.VMEM((16, M_ROWS, CH), BF16),
            pltpu.VMEM((16, M_ROWS, CH), BF16),
            pltpu.VMEM((16, M_ROWS, CH), F32),
            pltpu.VMEM((16, M_ROWS, CH), F32),
            pltpu.VMEM((2, 4, TILE, 128), F32),
            pltpu.VMEM((TILE, TILE, CH), BF16),
            pltpu.VMEM((9 * C_LAT, CH), BF16),
            pltpu.VMEM((4, CH), F32),
            pltpu.VMEM((16, CH, CH), BF16),
            pltpu.SemaphoreType.DMA((6,)),
            pltpu.SemaphoreType.DMA((N_BLOCK,)),
        ],
        compiler_params=pltpu.CompilerParams(vmem_limit_bytes=52 * MIB),
        name="main",
    )(
        place,
        recv,
        stats,
        hbm(taps),
        hbm(bias),
        hbm(norm_gain.reshape(1, CH)),
        hbm(norm_shift.reshape(1, CH)),
        hbm(mid_bias.reshape(1, CH)),
        hbm(points),
    )


def solution(mesh):
    in_specs = (P(None, ("row", "col")), P(), P(), P(), P(), P(), P())
    return jax.shard_map(
        step, mesh=mesh, in_specs=in_specs, out_specs=P("row", "col", None), check_vma=False
    )
```

```python
import functools

import jax
import jax.numpy as jnp
from jax import lax
from jax.experimental import pallas as pl
from jax.experimental.pallas import tpu as pltpu
from jax.sharding import PartitionSpec as P

C_LAT = 16
CH = 512
GROUPS = 32
TILE = 64
WIDTH = 1024
N_ROW = 8
N_COL = 16
N_DEV = N_ROW * N_COL
OWN = 4
ACT = TILE + 2
LAT = TILE + 4
PLANES = 6
EPSILON = 1e-06
BF16 = jnp.bfloat16
F32 = jnp.float32
VMEM = pl.BlockSpec(memory_space=pltpu.VMEM)
SMEM = pl.BlockSpec(memory_space=pltpu.SMEM)
HBM = pl.BlockSpec(memory_space=pltpu.HBM)
MIB = 1 << 20


def dot_tn(lhs, rhs):
    return lax.dot_general(lhs, rhs, (((0,), (0,)), ((), ())), preferred_element_type=F32)


def dot_nt(lhs, rhs):
    return lax.dot_general(lhs, rhs, (((1,), (1,)), ((), ())), preferred_element_type=F32)


def hbm(array):
    return pltpu.with_memory_space_constraint(array, pltpu.HBM)


def start_copies(sources, targets, sems):
    copies = [
        pltpu.make_async_copy(source, target, sems.at[i])
        for i, (source, target) in enumerate(zip(sources, targets))
    ]
    for copy in copies:
        copy.start()
    return copies


def pack_kernel(own_hbm, out, rows, own, sems):
    copies = start_copies((own_hbm,), (own,), sems)
    k = lax.broadcasted_iota(jnp.int32, (384, 256), 0)
    n = lax.broadcasted_iota(jnp.int32, (384, 256), 1)
    lane = n % 128
    column = 64 * (n // 128) + 4 * (lane % 16) + lane // 16 + 126
    pick = jnp.where(k == column, 1.0, 0.0).astype(BF16)
    zero = jnp.zeros((64, 128), BF16)
    copies[0].wait()
    for r in range(OWN):
        rows[16 * r : 16 * r + 16] = own[:, WIDTH * r : WIDTH * (r + 1)]
    for t in range(8):
        parts = [
            rows[:, 128 * u : 128 * (u + 1)] if 0 <= u < 8 else zero for u in (t - 1, t, t + 1)
        ]
        moved = jnp.dot(jnp.concatenate(parts, axis=1), pick, preferred_element_type=F32)
        out[2 * t] = moved[:, :128].astype(BF16)
        out[2 * t + 1] = moved[:, 128:].astype(BF16)


def add_cells(value, total, squares):
    value = value.reshape(value.shape[0] // 8, 8, CH)
    return total + jnp.sum(value, axis=0), squares + jnp.sum(value * value, axis=0)


def inner_kernel(recv, weight_hbm, bias_hbm, sums, pairs, weight, bias, sems):
    copies = start_copies((weight_hbm, bias_hbm), (weight, bias), sems)
    rows = recv[...].astype(F32)
    low = lax.broadcasted_iota(jnp.int32, (16 * (TILE - 1), 128), 1) < 64
    for b in range(3):
        even = pltpu.roll(rows, 112 - 16 * b, 1)
        odd = pltpu.roll(rows, (176 - 16 * b) % 128, 1)
        pairs[b] = jnp.where(low, even[:-16], odd[16:]).astype(BF16)
    for copy in copies:
        copy.wait()
    taps = weight[...]
    shift = bias[...]

    def accumulate(first, count, carry):
        patches = [
            jnp.concatenate(
                [
                    pairs[b, pl.ds(pl.multiple_of((2 * (first + j) + a) * 16, 16), 16)]
                    for a in range(3)
                    for b in range(3)
                ],
                axis=0,
            )
            for j in range(count)
        ]
        return add_cells(dot_tn(jnp.concatenate(patches, axis=1), taps) + shift, *carry)

    zero = jnp.zeros((8, CH), F32)
    carry = lax.fori_loop(0, 7, lambda i, c: accumulate(4 * i, 4, c), (zero, zero))
    sums[0], sums[1] = accumulate(28, 3, carry)


def rim_rows(place, rim):
    top = rim[jnp.maximum(place[0] - 1, 0)].astype(F32)
    bot = rim[jnp.minimum(place[0] + 1, N_ROW - 1)].astype(F32)
    top = jnp.where(place[0] == 0, 0.0, top)
    return top, jnp.where(place[0] == N_ROW - 1, 0.0, bot)


def outer_kernel(place, recv, rim, sums, weight_hbm, bias_hbm, out, weight, bias, sems):
    copies = start_copies((weight_hbm, bias_hbm), (weight, bias), sems)
    channel = lax.broadcasted_iota(jnp.int32, (CH, 128), 0) // (CH // GROUPS)
    lane = lax.broadcasted_iota(jnp.int32, (CH, 128), 1)
    to_sum = jnp.where(channel == lane, 1.0, 0.0)
    to_squares = jnp.where(channel == lane - GROUPS, 1.0, 0.0)
    top, bot = rim_rows(place, rim)
    first = jnp.concatenate([top[16:], recv[0:32].astype(F32)], axis=0)
    last = jnp.concatenate([recv[16 * TILE - 32 :].astype(F32), bot[:16]], axis=0)
    low = lax.broadcasted_iota(jnp.int32, (48, 128), 1) < 64
    shifted = [
        jnp.where(
            low, pltpu.roll(first, 112 - 16 * b, 1), pltpu.roll(last, (176 - 16 * b) % 128, 1)
        ).astype(BF16)
        for b in range(3)
    ]
    patch = jnp.concatenate(
        [shifted[b][16 * a : 16 * a + 16] for a in range(3) for b in range(3)], axis=0
    )
    for copy in copies:
        copy.wait()
    total, squares = add_cells(dot_tn(patch, weight[...]) + bias[...], sums[0], sums[1])
    exact = functools.partial(
        jnp.dot, precision=lax.Precision.HIGHEST, preferred_element_type=F32
    )
    both = exact(total, to_sum) + exact(squares, to_squares)
    out[...] = jnp.broadcast_to(jnp.sum(both, axis=0).reshape(1, 1, 128), (N_DEV, 1, 128))


def affine(stats, bias, gain, shift):
    sums = jnp.sum(stats[...], axis=0)
    sums = jnp.broadcast_to(sums, (8, 128)) / (TILE * TILE * N_DEV * (CH // GROUPS))
    channel = lax.broadcasted_iota(jnp.int32, (128, CH), 1) // (CH // GROUPS)
    lane = lax.broadcasted_iota(jnp.int32, (128, CH), 0)
    spread = functools.partial(
        jnp.dot, precision=lax.Precision.HIGHEST, preferred_element_type=F32
    )
    mean = spread(sums, jnp.where(channel == lane, 1.0, 0.0))[0:1]
    square = spread(sums, jnp.where(channel == lane - GROUPS, 1.0, 0.0))[0:1]
    scale = lax.rsqrt(square - mean * mean + EPSILON) * gain[...]
    return scale, (bias[...] - mean) * scale + shift[...]


def prepare_kernel(weight, points):
    def thirds(g):
        even = 0.5 * (g[0] + g[2])
        odd = 0.5 * g[1]
        return g[0], even + odd, even - odd, g[2]

    def transform(step, _):
        rows = pl.ds(pl.multiple_of(step * 16, 16), 16)
        for l in range(4):
            lanes = slice(128 * l, 128 * l + 128)
            columns = [
                thirds([weight[a, b, rows, lanes].astype(F32) for a in range(3)]) for b in range(3)
            ]
            for u in range(4):
                for v, value in enumerate(thirds([columns[b][u] for b in range(3)])):
                    points[4 * u + v, rows, lanes] = value.astype(BF16)
        return 0

    lax.fori_loop(0, weight.shape[2] // 16, transform, 0)


BLOCK = 8
TILES = 4
N_BLOCK = TILE // 2 // BLOCK
M_ROWS = BLOCK * 32


def main_kernel(
    place,
    recv,
    rim,
    stats,
    taps_hbm,
    bias_hbm,
    gain_hbm,
    shift_hbm,
    mid_bias_hbm,
    low_hbm,
    high_hbm,
    out_hbm,
    lat,
    act,
    affines,
    raw,
    v0,
    v1,
    m0,
    m1,
    spread,
    out,
    taps,
    vectors,
    points,
    in_sems,
    sems,
):
    loads = start_copies(
        (taps_hbm, bias_hbm, gain_hbm, shift_hbm, mid_bias_hbm, low_hbm, high_hbm),
        (
            taps,
            *(vectors.at[i : i + 1] for i in range(4)),
            points.at[:, : CH // 2],
            points.at[:, CH // 2 :],
        ),
        in_sems,
    )
    v_slots, m_slots = (v0, v1), (m0, m1)

    def place_rows(at, rows):
        for b in range(3):
            value = rows if b == 0 else pltpu.roll(rows, 128 - 16 * b, 1)
            lat[b, at : at + rows.shape[0]] = value.astype(BF16)

    top, bot = rim_rows(place, rim)
    place_rows(0, top)
    for r in range(0, 16 * TILE, 64):
        place_rows(32 + r, recv[r : r + 64].astype(F32))
    place_rows(32 + 16 * TILE, bot)
    for load in loads[:-2]:
        load.wait()
    scale, offset = affine(stats, vectors[0:1], vectors[1:2], vectors[2:3])
    cell = lax.broadcasted_iota(jnp.int32, (16, CH), 0)
    hide_low = jnp.logical_and(cell == 0, place[1] == 0)
    hide_high = jnp.logical_and(cell == 15, place[1] == N_COL - 1)
    for i, value in enumerate((0.5 * scale, 0.5 * offset)):
        wide = jnp.broadcast_to(value, (16, CH))
        affines[i, 0] = jnp.where(hide_low, 0.0, wide)
        affines[i, 1] = wide
        affines[i, 2] = jnp.where(hide_high, 0.0, wide)
        affines[i, 3] = jnp.zeros((16, CH), F32)

    def contract(pair):
        patches = []
        for j in range(2):
            at = pl.multiple_of((2 * pair + j) * 16, 16)
            patches.append(
                jnp.concatenate(
                    [lat[b, pl.ds(at + 16 * a, 16)] for a in range(3) for b in range(3)], axis=0
                )
            )
        raw[...] = dot_tn(jnp.concatenate(patches, axis=1), taps[...])

    def activate(pair, pieces=range(4)):
        for j in range(2):
            row = 2 * pair + j
            hidden = jnp.logical_or(
                jnp.logical_and(row == 0, place[0] == 0),
                jnp.logical_and(row == ACT - 1, place[0] == N_ROW - 1),
            )
            for l in pieces:
                lanes = slice(128 * l, 128 * l + 128)
                for t in range(PLANES):
                    kind = jnp.where(hidden, 3, 0 if t == 0 else (2 if t == PLANES - 1 else 1))
                    at = 128 * j + 16 * t
                    half = raw[at : at + 16, lanes] * affines[0, kind, :, lanes]
                    half = half + affines[1, kind, :, lanes]
                    act[row, l, 16 * t : 16 * t + 16] = (half + half * jnp.tanh(half)).astype(BF16)

    def build(tile, slot, pieces=range(4)):
        base = pl.multiple_of((tile % BLOCK) * 32, 32)
        for l in pieces:
            rows = []
            for q in range(2):
                for t in range(len(rows), 4 + 2 * q):
                    d = [act[2 * tile + u, l, 16 * t : 16 * t + 16] for u in range(4)]
                    rows.append((d[0] - d[2], d[1] + d[2], d[2] - d[1], d[1] - d[3]))
                for u in range(4):
                    r = [rows[2 * q + v][u] for v in range(4)]
                    columns = (r[0] - r[2], r[1] + r[2], r[2] - r[1], r[1] - r[3])
                    for v in range(4):
                        slot[4 * u + v, l, pl.ds(base + 16 * q, 16)] = columns[v]

    def multiply(point, v_slot, m_slot, half):
        cells = jnp.concatenate([v_slot[point, l] for l in range(4)], axis=1)
        value = dot_nt(cells, points[point, 256 * half : 256 * half + 256])
        for i in range(2):
            m_slot[point, 2 * half + i] = value[:, 128 * i : 128 * i + 128]

    def finish(tile, slot, pieces=range(4)):
        base = pl.multiple_of((tile % BLOCK) * 32, 32)
        for l in pieces:
            bias = vectors[3:4, 128 * l : 128 * l + 128]
            for q in range(2):
                for h in range(2):
                    sums = []
                    for u in range(4):
                        m = [slot[4 * u + v, l, pl.ds(base + 16 * q + 8 * h, 8)] for v in range(4)]
                        both, apart = m[1] + m[2], m[1] - m[2]
                        sums.append((m[0] + both, apart - m[3]))
                    for f in range(2):
                        z = [sums[u][f] for u in range(4)]
                        both, apart = z[1] + z[2], z[1] - z[2]
                        at = pl.ds(32 * h + 2 * q + f, 8, stride=4)
                        spread[0, l, at] = z[0] + both + bias
                        spread[1, l, at] = apart - z[3] + bias
            for e in range(2):
                out[2 * tile + e, l] = spread[e, l].astype(BF16)

    for pair in range(2):
        contract(pair)
        activate(pair)

    def warm(c, _):
        contract(c + 2)
        build(c, v0)
        activate(c + 2)
        return 0

    lax.fori_loop(0, BLOCK, warm, 0)
    loads[-2].wait()
    loads[-1].wait()
    last_pair = ACT // 2 - 1
    copies = []
    for n in range(N_BLOCK):
        this_v, next_v = v_slots[n % 2], v_slots[1 - n % 2]
        this_m, last_m = m_slots[n % 2], m_slots[1 - n % 2]

        def steady(c, _, n=n, this_v=this_v, next_v=next_v, this_m=this_m, last_m=last_m):
            first = n * BLOCK + c * TILES
            ahead = n < N_BLOCK - 1
            for k in range(TILES):
                g = first + k
                pair = jnp.minimum(g + BLOCK + 2, last_pair)
                if ahead:
                    contract(pair)
                for i in range(4):
                    multiply(2 * (c * TILES + k) + i // 2, this_v, this_m, i % 2)
                    if n > 0:
                        finish(g - BLOCK, last_m, (i,))
                    if ahead:
                        build(g + BLOCK, next_v, (i,))
                        activate(pair, (i,))
            return 0

        lax.fori_loop(0, BLOCK // TILES, steady, 0)
        if n > 0:
            copies.extend(send(out, out_hbm, n - 1, sems))

    def drain(c, _):
        finish((N_BLOCK - 1) * BLOCK + c, m_slots[1 - N_BLOCK % 2])
        return 0

    lax.fori_loop(0, BLOCK, drain, 0)
    copies.extend(send(out, out_hbm, N_BLOCK - 1, sems))
    for copy in copies:
        copy.wait()


def send(out, out_hbm, n, sems):
    rows = slice(2 * BLOCK * n, 2 * BLOCK * (n + 1))
    copies = [
        pltpu.make_async_copy(
            out.at[rows, l], out_hbm.at[rows, :, 128 * l : 128 * l + 128], sems.at[n, l]
        )
        for l in range(4)
    ]
    for copy in copies:
        copy.start()
    return copies


def step(latent, in_weight, in_bias, norm_gain, norm_shift, mid_weight, mid_bias):
    both = ("row", "col")
    taps = in_weight.reshape(9 * C_LAT, CH)
    bias = in_bias.reshape(1, CH)
    place = jnp.stack([lax.axis_index("row"), lax.axis_index("col")]).astype(jnp.int32)
    weights = [pltpu.VMEM((9 * C_LAT, CH), BF16), pltpu.VMEM((1, CH), F32)]
    small = pltpu.CompilerParams(vmem_limit_bytes=12 * MIB)
    chunks = pl.pallas_call(
        pack_kernel,
        out_shape=jax.ShapeDtypeStruct((N_COL, 64, 128), BF16),
        in_specs=[HBM],
        out_specs=VMEM,
        scratch_shapes=[
            pltpu.VMEM((64, WIDTH), BF16),
            pltpu.VMEM((C_LAT, OWN * WIDTH), BF16),
            pltpu.SemaphoreType.DMA((1,)),
        ],
        compiler_params=small,
        name="pack",
    )(hbm(latent))
    recv = lax.all_to_all(chunks, "col", split_axis=0, concat_axis=0, tiled=True)
    recv = recv.reshape(16 * TILE, 128)
    above = lax.broadcasted_iota(jnp.int32, (N_ROW, 32, 128), 0) > place[0]
    edges = jnp.where(above, recv[None, -32:], recv[None, :32])
    rim = lax.all_to_all(edges, "row", split_axis=0, concat_axis=0, tiled=True)
    sums = pl.pallas_call(
        inner_kernel,
        out_shape=jax.ShapeDtypeStruct((2, 8, CH), F32),
        in_specs=[VMEM, HBM, HBM],
        out_specs=VMEM,
        scratch_shapes=[pltpu.VMEM((3, 16 * (TILE - 1), 128), BF16)]
        + weights
        + [pltpu.SemaphoreType.DMA((2,))],
        compiler_params=small,
        name="inner",
    )(recv, hbm(taps), hbm(bias))
    partial = pl.pallas_call(
        outer_kernel,
        out_shape=jax.ShapeDtypeStruct((N_DEV, 1, 128), F32),
        in_specs=[SMEM, VMEM, VMEM, VMEM, HBM, HBM],
        out_specs=VMEM,
        scratch_shapes=weights + [pltpu.SemaphoreType.DMA((2,))],
        compiler_params=small,
        name="outer",
    )(place, recv, rim, sums, hbm(taps), hbm(bias))
    stats = lax.all_to_all(partial, both, split_axis=0, concat_axis=0, tiled=True)
    weight = hbm(jnp.transpose(mid_weight, (1, 2, 0, 3)))
    points = []
    for part in range(2):
        points.append(
            pl.pallas_call(
                prepare_kernel,
                out_shape=jax.ShapeDtypeStruct((16, CH // 2, CH), BF16),
                grid=(4,),
                in_specs=[
                    pl.BlockSpec((3, 3, CH // 8, CH), lambda i, part=part: (0, 0, i + 4 * part, 0))
                ],
                out_specs=pl.BlockSpec((16, CH // 8, CH), lambda i: (0, i, 0)),
                compiler_params=pltpu.CompilerParams(vmem_limit_bytes=60 * MIB),
            )(weight)
        )
    return pl.pallas_call(
        main_kernel,
        out_shape=jax.ShapeDtypeStruct((TILE, TILE, CH), BF16),
        in_specs=[SMEM, VMEM, VMEM, VMEM] + [HBM] * 7,
        out_specs=HBM,
        scratch_shapes=[
            pltpu.VMEM((3, LAT * 16, 128), BF16),
            pltpu.VMEM((ACT, 4, PLANES * 16, 128), BF16),
            pltpu.VMEM((2, 4, 16, CH), F32),
            pltpu.VMEM((256, CH), F32),
            pltpu.VMEM((16, 4, M_ROWS, 128), BF16),
            pltpu.VMEM((16, 4, M_ROWS, 128), BF16),
            pltpu.VMEM((16, 4, M_ROWS, 128), F32),
            pltpu.VMEM((16, 4, M_ROWS, 128), F32),
            pltpu.VMEM((2, 4, TILE, 128), F32),
            pltpu.VMEM((TILE, 4, TILE, 128), BF16),
            pltpu.VMEM((9 * C_LAT, CH), BF16),
            pltpu.VMEM((4, CH), F32),
            pltpu.VMEM((16, CH, CH), BF16),
            pltpu.SemaphoreType.DMA((7,)),
            pltpu.SemaphoreType.DMA((N_BLOCK, 4)),
        ],
        compiler_params=pltpu.CompilerParams(vmem_limit_bytes=52 * MIB),
        name="main",
    )(
        place,
        recv,
        rim,
        stats,
        hbm(taps),
        hbm(bias),
        hbm(norm_gain.reshape(1, CH)),
        hbm(norm_shift.reshape(1, CH)),
        hbm(mid_bias.reshape(1, CH)),
        hbm(points[0]),
        hbm(points[1]),
    )


def solution(mesh):
    in_specs = (P(None, ("row", "col")), P(), P(), P(), P(), P(), P())
    return jax.shard_map(
        step, mesh=mesh, in_specs=in_specs, out_specs=P("row", "col", None), check_vma=False
    )
```

```python
import functools

import jax
import jax.numpy as jnp
from jax import lax
from jax.experimental import pallas as pl
from jax.experimental.pallas import tpu as pltpu
from jax.sharding import PartitionSpec as P

C_LAT = 16
CH = 512
GROUPS = 32
TILE = 64
WIDTH = 1024
N_ROW = 8
N_COL = 16
N_DEV = N_ROW * N_COL
OWN = 4
ACT = TILE + 2
LAT = TILE + 4
PLANES = 6
EPSILON = 1e-06
BF16 = jnp.bfloat16
F32 = jnp.float32
VMEM = pl.BlockSpec(memory_space=pltpu.VMEM)
SMEM = pl.BlockSpec(memory_space=pltpu.SMEM)
HBM = pl.BlockSpec(memory_space=pltpu.HBM)
MIB = 1 << 20


def dot_tn(lhs, rhs):
    return lax.dot_general(lhs, rhs, (((0,), (0,)), ((), ())), preferred_element_type=F32)


def dot_nt(lhs, rhs):
    return lax.dot_general(lhs, rhs, (((1,), (1,)), ((), ())), preferred_element_type=F32)


def hbm(array):
    return pltpu.with_memory_space_constraint(array, pltpu.HBM)


def start_copies(sources, targets, sems):
    copies = [
        pltpu.make_async_copy(source, target, sems.at[i])
        for i, (source, target) in enumerate(zip(sources, targets))
    ]
    for copy in copies:
        copy.start()
    return copies


def pack_kernel(own, out, rows):
    k = lax.broadcasted_iota(jnp.int32, (384, 256), 0)
    n = lax.broadcasted_iota(jnp.int32, (384, 256), 1)
    lane = n % 128
    column = 64 * (n // 128) + 4 * (lane % 16) + lane // 16 + 126
    pick = jnp.where(k == column, 1.0, 0.0).astype(BF16)
    zero = jnp.zeros((64, 128), BF16)
    for r in range(OWN):
        rows[16 * r : 16 * r + 16] = own[:, WIDTH * r : WIDTH * (r + 1)]
    for t in range(8):
        parts = [
            rows[:, 128 * u : 128 * (u + 1)] if 0 <= u < 8 else zero for u in (t - 1, t, t + 1)
        ]
        moved = jnp.dot(jnp.concatenate(parts, axis=1), pick, preferred_element_type=F32)
        out[2 * t] = moved[:, :128].astype(BF16)
        out[2 * t + 1] = moved[:, 128:].astype(BF16)


def add_cells(value, total, squares):
    value = value.reshape(value.shape[0] // 8, 8, CH)
    return total + jnp.sum(value, axis=0), squares + jnp.sum(value * value, axis=0)


def inner_kernel(
    recv, weight_hbm, bias_hbm, gain_hbm, shift_hbm, mid_bias_hbm, sums, weight, vectors, pairs, sems
):
    copies = start_copies(
        (weight_hbm, bias_hbm, gain_hbm, shift_hbm, mid_bias_hbm),
        (weight, *(vectors.at[i : i + 1] for i in range(4))),
        sems,
    )
    rows = recv[...].astype(F32)
    low = lax.broadcasted_iota(jnp.int32, (16 * (TILE - 1), 128), 1) < 64
    for b in range(3):
        even = pltpu.roll(rows, 112 - 16 * b, 1)
        odd = pltpu.roll(rows, (176 - 16 * b) % 128, 1)
        pairs[b] = jnp.where(low, even[:-16], odd[16:]).astype(BF16)
    for copy in copies:
        copy.wait()

    def contract(first, count):
        patches = [
            jnp.concatenate(
                [
                    pairs[b, pl.ds(pl.multiple_of((2 * (first + j) + a) * 16, 16), 16)]
                    for a in range(3)
                    for b in range(3)
                ],
                axis=0,
            )
            for j in range(count)
        ]
        return dot_tn(jnp.concatenate(patches, axis=1), weight[...])

    def accumulate(i, carry):
        values = [contract(GANG * i + 4 * part, 4) for part in range(GANG // 4)]
        for value in values:
            carry = add_cells(value, *carry)
        return carry

    zero = jnp.zeros((8, CH), F32)
    whole = 28 // GANG
    carry = lax.fori_loop(0, whole, accumulate, (zero, zero))
    sums[0], sums[1] = add_cells(contract(28, 3), *carry)


GANG = 28


def rim_rows(place, rim):
    top = rim[jnp.maximum(place[0] - 1, 0)].astype(F32)
    bot = rim[jnp.minimum(place[0] + 1, N_ROW - 1)].astype(F32)
    top = jnp.where(place[0] == 0, 0.0, top)
    return top, jnp.where(place[0] == N_ROW - 1, 0.0, bot)


def outer_kernel(place, recv, rim, sums, weight, vectors, out):
    channel = lax.broadcasted_iota(jnp.int32, (CH, 128), 0) // (CH // GROUPS)
    lane = lax.broadcasted_iota(jnp.int32, (CH, 128), 1)
    to_sum = jnp.where(channel == lane, 1.0, 0.0)
    to_squares = jnp.where(channel == lane - GROUPS, 1.0, 0.0)
    top, bot = rim_rows(place, rim)
    first = jnp.concatenate([top[16:], recv[0:32].astype(F32)], axis=0)
    last = jnp.concatenate([recv[16 * TILE - 32 :].astype(F32), bot[:16]], axis=0)
    low = lax.broadcasted_iota(jnp.int32, (48, 128), 1) < 64
    shifted = [
        jnp.where(
            low, pltpu.roll(first, 112 - 16 * b, 1), pltpu.roll(last, (176 - 16 * b) % 128, 1)
        ).astype(BF16)
        for b in range(3)
    ]
    patch = jnp.concatenate(
        [shifted[b][16 * a : 16 * a + 16] for a in range(3) for b in range(3)], axis=0
    )
    total, squares = add_cells(dot_tn(patch, weight[...]), sums[0], sums[1])
    bias = vectors[0:1]
    cells = TILE * TILE // 8
    squares = squares + bias * (2.0 * total + cells * bias)
    total = total + cells * bias
    exact = functools.partial(
        jnp.dot, precision=lax.Precision.HIGHEST, preferred_element_type=F32
    )
    both = exact(total, to_sum) + exact(squares, to_squares)
    out[...] = jnp.broadcast_to(jnp.sum(both, axis=0).reshape(1, 1, 128), (N_DEV, 1, 128))


def affine(stats, bias, gain, shift):
    sums = jnp.sum(stats[...], axis=0)
    sums = jnp.broadcast_to(sums, (8, 128)) / (TILE * TILE * N_DEV * (CH // GROUPS))
    channel = lax.broadcasted_iota(jnp.int32, (128, CH), 1) // (CH // GROUPS)
    lane = lax.broadcasted_iota(jnp.int32, (128, CH), 0)
    spread = functools.partial(
        jnp.dot, precision=lax.Precision.HIGHEST, preferred_element_type=F32
    )
    mean = spread(sums, jnp.where(channel == lane, 1.0, 0.0))[0:1]
    square = spread(sums, jnp.where(channel == lane - GROUPS, 1.0, 0.0))[0:1]
    scale = lax.rsqrt(square - mean * mean + EPSILON) * gain[...]
    return scale, (bias[...] - mean) * scale + shift[...]


def prepare_kernel(weight, points):
    def thirds(g):
        even = 0.5 * (g[0] + g[2])
        odd = 0.5 * g[1]
        return g[0], even + odd, even - odd, g[2]

    def transform(step, _):
        rows = pl.ds(pl.multiple_of(step * 16, 16), 16)
        for l in range(4):
            lanes = slice(128 * l, 128 * l + 128)
            columns = [
                thirds([weight[a, b, rows, lanes].astype(F32) for a in range(3)]) for b in range(3)
            ]
            for u in range(4):
                for v, value in enumerate(thirds([columns[b][u] for b in range(3)])):
                    points[4 * u + v, rows, lanes] = value.astype(BF16)
        return 0

    lax.fori_loop(0, weight.shape[2] // 16, transform, 0)


BLOCK = 8
TILES = 4
N_BLOCK = TILE // 2 // BLOCK
M_ROWS = BLOCK * 32


def main_kernel(
    place,
    recv,
    rim,
    stats,
    taps,
    vectors,
    low_hbm,
    high_hbm,
    out_hbm,
    lat,
    act,
    affines,
    raw,
    v0,
    v1,
    m0,
    m1,
    spread,
    out,
    points,
    in_sems,
    sems,
):
    loads = start_copies(
        (low_hbm, high_hbm), (points.at[:, : CH // 2], points.at[:, CH // 2 :]), in_sems
    )

    v_slots, m_slots = (v0, v1), (m0, m1)

    def place_rows(at, rows):
        for b in range(3):
            value = rows if b == 0 else pltpu.roll(rows, 128 - 16 * b, 1)
            lat[b, at : at + rows.shape[0]] = value.astype(BF16)

    top, bot = rim_rows(place, rim)
    place_rows(0, top)
    for r in range(0, 16 * TILE, 64):
        place_rows(32 + r, recv[r : r + 64].astype(F32))
    place_rows(32 + 16 * TILE, bot)
    scale, offset = affine(stats, vectors[0:1], vectors[1:2], vectors[2:3])
    cell = lax.broadcasted_iota(jnp.int32, (16, CH), 0)
    hide_low = jnp.logical_and(cell == 0, place[1] == 0)
    hide_high = jnp.logical_and(cell == 15, place[1] == N_COL - 1)
    for i, value in enumerate((0.5 * scale, 0.5 * offset)):
        wide = jnp.broadcast_to(value, (16, CH))
        affines[i, 0] = jnp.where(hide_low, 0.0, wide)
        affines[i, 1] = wide
        affines[i, 2] = jnp.where(hide_high, 0.0, wide)
        affines[i, 3] = jnp.zeros((16, CH), F32)

    def contract(pair):
        patches = []
        for j in range(2):
            at = pl.multiple_of((2 * pair + j) * 16, 16)
            patches.append(
                jnp.concatenate(
                    [lat[b, pl.ds(at + 16 * a, 16)] for a in range(3) for b in range(3)], axis=0
                )
            )
        return dot_tn(jnp.concatenate(patches, axis=1), taps[...])

    def activate(pair, raw, pieces=range(4)):
        for j in range(2):
            row = 2 * pair + j
            hidden = jnp.logical_or(
                jnp.logical_and(row == 0, place[0] == 0),
                jnp.logical_and(row == ACT - 1, place[0] == N_ROW - 1),
            )
            for l in pieces:
                lanes = slice(128 * l, 128 * l + 128)
                for t in range(PLANES):
                    kind = jnp.where(hidden, 3, 0 if t == 0 else (2 if t == PLANES - 1 else 1))
                    at = 128 * j + 16 * t
                    half = raw[at : at + 16, lanes] * affines[0, kind, :, lanes]
                    half = half + affines[1, kind, :, lanes]
                    act[row, l, 16 * t : 16 * t + 16] = (half + half * jnp.tanh(half)).astype(BF16)

    def build(tile, slot, pieces=range(4)):
        base = pl.multiple_of((tile % BLOCK) * 32, 32)
        for l in pieces:
            rows = []
            for q in range(2):
                for t in range(len(rows), 4 + 2 * q):
                    d = [act[2 * tile + u, l, 16 * t : 16 * t + 16] for u in range(4)]
                    rows.append((d[0] - d[2], d[1] + d[2], d[2] - d[1], d[1] - d[3]))
                for u in range(4):
                    r = [rows[2 * q + v][u] for v in range(4)]
                    columns = (r[0] - r[2], r[1] + r[2], r[2] - r[1], r[1] - r[3])
                    for v in range(4):
                        slot[4 * u + v, l, pl.ds(base + 16 * q, 16)] = columns[v]

    def multiply(point, v_slot, m_slot, half):
        cells = jnp.concatenate([v_slot[point, l] for l in range(4)], axis=1)
        value = dot_nt(cells, points[point, 256 * half : 256 * half + 256])
        for i in range(2):
            m_slot[point, 2 * half + i] = value[:, 128 * i : 128 * i + 128]

    def finish(tile, slot, pieces=range(4)):
        base = pl.multiple_of((tile % BLOCK) * 32, 32)
        for l in pieces:
            bias = vectors[3:4, 128 * l : 128 * l + 128]
            for q in range(2):
                for h in range(2):
                    sums = []
                    for u in range(4):
                        m = [slot[4 * u + v, l, pl.ds(base + 16 * q + 8 * h, 8)] for v in range(4)]
                        both, apart = m[1] + m[2], m[1] - m[2]
                        sums.append((m[0] + both, apart - m[3]))
                    for f in range(2):
                        z = [sums[u][f] for u in range(4)]
                        both, apart = z[1] + z[2], z[1] - z[2]
                        at = pl.ds(32 * h + 2 * q + f, 8, stride=4)
                        spread[0, l, at] = z[0] + both + bias
                        spread[1, l, at] = apart - z[3] + bias
            for e in range(2):
                out[2 * tile + e, l] = spread[e, l].astype(BF16)

    for pair in range(2):
        activate(pair, contract(pair))

    def warm(c, _):
        value = contract(c + 2)
        build(c, v0)
        activate(c + 2, value)
        return 0

    lax.fori_loop(0, BLOCK, warm, 0)
    for load in loads:
        load.wait()
    last_pair = ACT // 2 - 1
    copies = []
    for n in range(N_BLOCK):
        this_v, next_v = v_slots[n % 2], v_slots[1 - n % 2]
        this_m, last_m = m_slots[n % 2], m_slots[1 - n % 2]

        def steady(c, _, n=n, this_v=this_v, next_v=next_v, this_m=this_m, last_m=last_m):
            first = n * BLOCK + c * TILES
            ahead = n < N_BLOCK - 1
            for k in range(TILES):
                g = first + k
                pair = jnp.minimum(g + BLOCK + 2, last_pair)
                if ahead:
                    value = contract(pair)
                for i in range(4):
                    multiply(2 * (c * TILES + k) + i // 2, this_v, this_m, i % 2)
                    if n > 0:
                        finish(g - BLOCK, last_m, (i,))
                    if ahead:
                        build(g + BLOCK, next_v, (i,))
                        activate(pair, value, (i,))
            return 0

        lax.fori_loop(0, BLOCK // TILES, steady, 0)
        if n > 0:
            copies.extend(send(out, out_hbm, n - 1, sems))

    def drain(c, _):
        finish((N_BLOCK - 1) * BLOCK + c, m_slots[1 - N_BLOCK % 2])
        return 0

    for half in range(2):
        lax.fori_loop(half * BLOCK // 2, (half + 1) * BLOCK // 2, drain, 0)
        copies.extend(send(out, out_hbm, N_BLOCK - 1 + half, sems, half))
    for copy in copies:
        copy.wait()


def send(out, out_hbm, n, sems, half=None):
    rows = slice(2 * BLOCK * n, 2 * BLOCK * (n + 1))
    if half is not None:
        first = 2 * BLOCK * (N_BLOCK - 1) + BLOCK * half
        rows = slice(first, first + BLOCK)
    copies = [
        pltpu.make_async_copy(
            out.at[rows, l], out_hbm.at[rows, :, 128 * l : 128 * l + 128], sems.at[n, l]
        )
        for l in range(4)
    ]
    for copy in copies:
        copy.start()
    return copies


def step(latent, in_weight, in_bias, norm_gain, norm_shift, mid_weight, mid_bias):
    both = ("row", "col")
    place = jnp.stack([lax.axis_index("row"), lax.axis_index("col")]).astype(jnp.int32)
    small = pltpu.CompilerParams(vmem_limit_bytes=12 * MIB)
    chunks = pl.pallas_call(
        pack_kernel,
        out_shape=jax.ShapeDtypeStruct((N_COL, 64, 128), BF16),
        in_specs=[VMEM],
        out_specs=VMEM,
        scratch_shapes=[pltpu.VMEM((64, WIDTH), BF16)],
        compiler_params=small,
        name="pack",
    )(latent)
    recv = lax.all_to_all(chunks, "col", split_axis=0, concat_axis=0, tiled=True)
    recv = recv.reshape(16 * TILE, 128)
    above = lax.broadcasted_iota(jnp.int32, (N_ROW, 32, 128), 0) > place[0]
    edges = jnp.where(above, recv[None, -32:], recv[None, :32])
    rim = lax.all_to_all(edges, "row", split_axis=0, concat_axis=0, tiled=True)
    sums, taps, vectors = pl.pallas_call(
        inner_kernel,
        out_shape=[
            jax.ShapeDtypeStruct((2, 8, CH), F32),
            jax.ShapeDtypeStruct((9 * C_LAT, CH), BF16),
            jax.ShapeDtypeStruct((4, CH), F32),
        ],
        in_specs=[VMEM] + [HBM] * 5,
        out_specs=[VMEM] * 3,
        scratch_shapes=[pltpu.VMEM((3, 16 * (TILE - 1), 128), BF16), pltpu.SemaphoreType.DMA((5,))],
        compiler_params=small,
        name="inner",
    )(
        recv,
        hbm(in_weight.reshape(9 * C_LAT, CH)),
        *(hbm(v.reshape(1, CH)) for v in (in_bias, norm_gain, norm_shift, mid_bias)),
    )
    partial = pl.pallas_call(
        outer_kernel,
        out_shape=jax.ShapeDtypeStruct((N_DEV, 1, 128), F32),
        in_specs=[SMEM] + [VMEM] * 5,
        out_specs=VMEM,
        compiler_params=small,
        name="outer",
    )(place, recv, rim, sums, taps, vectors)
    stats = lax.all_to_all(partial, both, split_axis=0, concat_axis=0, tiled=True)
    weight = hbm(jnp.transpose(mid_weight, (1, 2, 0, 3)))
    points = []
    for part in range(2):
        points.append(
            pl.pallas_call(
                prepare_kernel,
                out_shape=jax.ShapeDtypeStruct((16, CH // 2, CH), BF16),
                grid=(2,),
                in_specs=[
                    pl.BlockSpec((3, 3, CH // 4, CH), lambda i, part=part: (0, 0, i + 2 * part, 0))
                ],
                out_specs=pl.BlockSpec((16, CH // 4, CH), lambda i: (0, i, 0)),
                compiler_params=pltpu.CompilerParams(vmem_limit_bytes=60 * MIB),
            )(weight)
        )
    return pl.pallas_call(
        main_kernel,
        out_shape=jax.ShapeDtypeStruct((TILE, TILE, CH), BF16),
        in_specs=[SMEM] + [VMEM] * 5 + [HBM] * 2,
        out_specs=HBM,
        scratch_shapes=[
            pltpu.VMEM((3, LAT * 16, 128), BF16),
            pltpu.VMEM((ACT, 4, PLANES * 16, 128), BF16),
            pltpu.VMEM((2, 4, 16, CH), F32),
            pltpu.VMEM((256, CH), F32),
            pltpu.VMEM((16, 4, M_ROWS, 128), BF16),
            pltpu.VMEM((16, 4, M_ROWS, 128), BF16),
            pltpu.VMEM((16, 4, M_ROWS, 128), F32),
            pltpu.VMEM((16, 4, M_ROWS, 128), F32),
            pltpu.VMEM((2, 4, TILE, 128), F32),
            pltpu.VMEM((TILE, 4, TILE, 128), BF16),
            pltpu.VMEM((16, CH, CH), BF16),
            pltpu.SemaphoreType.DMA((2,)),
            pltpu.SemaphoreType.DMA((N_BLOCK + 1, 4)),
        ],
        compiler_params=pltpu.CompilerParams(vmem_limit_bytes=52 * MIB),
        name="main",
    )(
        place,
        recv,
        rim,
        stats,
        taps,
        vectors,
        hbm(points[0]),
        hbm(points[1]),
    )


def solution(mesh):
    in_specs = (P(None, ("row", "col")), P(), P(), P(), P(), P(), P())
    return jax.shard_map(
        step, mesh=mesh, in_specs=in_specs, out_specs=P("row", "col", None), check_vma=False
    )
```

```python
import functools

import jax
import jax.numpy as jnp
from jax import lax
from jax.experimental import pallas as pl
from jax.experimental.pallas import tpu as pltpu
from jax.sharding import PartitionSpec as P

C_LAT = 16
CH = 512
GROUPS = 32
TILE = 64
WIDTH = 1024
N_ROW = 8
N_COL = 16
N_DEV = N_ROW * N_COL
OWN = 4
ACT = TILE + 2
LAT = TILE + 4
PLANES = 6
EPSILON = 1e-06
BF16 = jnp.bfloat16
F32 = jnp.float32
VMEM = pl.BlockSpec(memory_space=pltpu.VMEM)
SMEM = pl.BlockSpec(memory_space=pltpu.SMEM)
HBM = pl.BlockSpec(memory_space=pltpu.HBM)
MIB = 1 << 20


def dot_tn(lhs, rhs):
    return lax.dot_general(lhs, rhs, (((0,), (0,)), ((), ())), preferred_element_type=F32)


def dot_nt(lhs, rhs):
    return lax.dot_general(lhs, rhs, (((1,), (1,)), ((), ())), preferred_element_type=F32)


def hbm(array):
    return pltpu.with_memory_space_constraint(array, pltpu.HBM)


def start_copies(sources, targets, sems):
    copies = [
        pltpu.make_async_copy(source, target, sems.at[i])
        for i, (source, target) in enumerate(zip(sources, targets))
    ]
    for copy in copies:
        copy.start()
    return copies


def pack_kernel(own, out, rows):
    k = lax.broadcasted_iota(jnp.int32, (384, 256), 0)
    n = lax.broadcasted_iota(jnp.int32, (384, 256), 1)
    lane = n % 128
    column = 64 * (n // 128) + 4 * (lane % 16) + lane // 16 + 126
    pick = jnp.where(k == column, 1.0, 0.0).astype(BF16)
    zero = jnp.zeros((64, 128), BF16)
    for r in range(OWN):
        rows[16 * r : 16 * r + 16] = own[:, WIDTH * r : WIDTH * (r + 1)]
    for t in range(8):
        parts = [
            rows[:, 128 * u : 128 * (u + 1)] if 0 <= u < 8 else zero for u in (t - 1, t, t + 1)
        ]
        moved = jnp.dot(jnp.concatenate(parts, axis=1), pick, preferred_element_type=F32)
        out[2 * t] = moved[:, :128].astype(BF16)
        out[2 * t + 1] = moved[:, 128:].astype(BF16)


def add_cells(value, total, squares):
    value = value.reshape(value.shape[0] // 8, 8, CH)
    return total + jnp.sum(value, axis=0), squares + jnp.sum(value * value, axis=0)


def inner_kernel(
    recv, weight_hbm, bias_hbm, gain_hbm, shift_hbm, mid_bias_hbm, sums, weight, vectors, pairs, sems
):
    copies = start_copies(
        (weight_hbm, bias_hbm, gain_hbm, shift_hbm, mid_bias_hbm),
        (weight, *(vectors.at[i : i + 1] for i in range(4))),
        sems,
    )
    rows = recv[...].astype(F32)
    low = lax.broadcasted_iota(jnp.int32, (16 * (TILE - 1), 128), 1) < 64
    for b in range(3):
        even = pltpu.roll(rows, 112 - 16 * b, 1)
        odd = pltpu.roll(rows, (176 - 16 * b) % 128, 1)
        pairs[b] = jnp.where(low, even[:-16], odd[16:]).astype(BF16)
    for copy in copies:
        copy.wait()

    def contract(first, count):
        patches = [
            jnp.concatenate(
                [
                    pairs[b, pl.ds(pl.multiple_of((2 * (first + j) + a) * 16, 16), 16)]
                    for a in range(3)
                    for b in range(3)
                ],
                axis=0,
            )
            for j in range(count)
        ]
        return dot_tn(jnp.concatenate(patches, axis=1), weight[...])

    def accumulate(i, carry):
        values = [contract(GANG * i + 4 * part, 4) for part in range(GANG // 4)]
        for value in values:
            carry = add_cells(value, *carry)
        return carry

    zero = jnp.zeros((8, CH), F32)
    whole = 28 // GANG
    carry = lax.fori_loop(0, whole, accumulate, (zero, zero))
    sums[0], sums[1] = add_cells(contract(28, 3), *carry)


GANG = 28


def rim_rows(place, rim):
    top = rim[jnp.maximum(place[0] - 1, 0)].astype(F32)
    bot = rim[jnp.minimum(place[0] + 1, N_ROW - 1)].astype(F32)
    top = jnp.where(place[0] == 0, 0.0, top)
    return top, jnp.where(place[0] == N_ROW - 1, 0.0, bot)


def outer_kernel(place, recv, rim, sums, weight, vectors, out):
    channel = lax.broadcasted_iota(jnp.int32, (CH, 128), 0) // (CH // GROUPS)
    lane = lax.broadcasted_iota(jnp.int32, (CH, 128), 1)
    to_sum = jnp.where(channel == lane, 1.0, 0.0)
    to_squares = jnp.where(channel == lane - GROUPS, 1.0, 0.0)
    top, bot = rim_rows(place, rim)
    first = jnp.concatenate([top[16:], recv[0:32].astype(F32)], axis=0)
    last = jnp.concatenate([recv[16 * TILE - 32 :].astype(F32), bot[:16]], axis=0)
    low = lax.broadcasted_iota(jnp.int32, (48, 128), 1) < 64
    shifted = [
        jnp.where(
            low, pltpu.roll(first, 112 - 16 * b, 1), pltpu.roll(last, (176 - 16 * b) % 128, 1)
        ).astype(BF16)
        for b in range(3)
    ]
    patch = jnp.concatenate(
        [shifted[b][16 * a : 16 * a + 16] for a in range(3) for b in range(3)], axis=0
    )
    total, squares = add_cells(dot_tn(patch, weight[...]), sums[0], sums[1])
    bias = vectors[0:1]
    cells = TILE * TILE // 8
    squares = squares + bias * (2.0 * total + cells * bias)
    total = total + cells * bias
    exact = functools.partial(
        jnp.dot, precision=lax.Precision.HIGHEST, preferred_element_type=F32
    )
    both = exact(total, to_sum) + exact(squares, to_squares)
    out[...] = jnp.broadcast_to(jnp.sum(both, axis=0).reshape(1, 1, 128), (N_DEV, 1, 128))


def affine(stats, bias, gain, shift):
    sums = jnp.sum(stats[...], axis=0)
    sums = jnp.broadcast_to(sums, (8, 128)) / (TILE * TILE * N_DEV * (CH // GROUPS))
    channel = lax.broadcasted_iota(jnp.int32, (128, CH), 1) // (CH // GROUPS)
    lane = lax.broadcasted_iota(jnp.int32, (128, CH), 0)
    spread = functools.partial(
        jnp.dot, precision=lax.Precision.HIGHEST, preferred_element_type=F32
    )
    mean = spread(sums, jnp.where(channel == lane, 1.0, 0.0))[0:1]
    square = spread(sums, jnp.where(channel == lane - GROUPS, 1.0, 0.0))[0:1]
    scale = lax.rsqrt(square - mean * mean + EPSILON) * gain[...]
    return scale, (bias[...] - mean) * scale + shift[...]


def prepare_kernel(weight, points):
    def thirds(g):
        even = 0.5 * (g[0] + g[2])
        odd = 0.5 * g[1]
        return g[0], even + odd, even - odd, g[2]

    def transform(step, _):
        rows = pl.ds(pl.multiple_of(step * 16, 16), 16)
        for l in range(4):
            lanes = slice(128 * l, 128 * l + 128)
            columns = [
                thirds([weight[a, b, rows, lanes].astype(F32) for a in range(3)]) for b in range(3)
            ]
            for u in range(4):
                for v, value in enumerate(thirds([columns[b][u] for b in range(3)])):
                    points[4 * u + v, rows, lanes] = value.astype(BF16)
        return 0

    lax.fori_loop(0, weight.shape[2] // 16, transform, 0)


BLOCK = 8
TILES = 4
N_BLOCK = TILE // 2 // BLOCK
M_ROWS = BLOCK * 32


def main_kernel(
    place,
    recv,
    rim,
    stats,
    taps,
    vectors,
    low_hbm,
    high_hbm,
    out_hbm,
    lat,
    act,
    affines,
    raw,
    v0,
    v1,
    m0,
    m1,
    spread,
    out,
    points,
    in_sems,
    sems,
):
    loads = start_copies(
        (low_hbm, high_hbm), (points.at[:, : CH // 2], points.at[:, CH // 2 :]), in_sems
    )

    v_slots, m_slots = (v0, v1), (m0, m1)

    def place_rows(at, rows):
        for b in range(3):
            value = rows if b == 0 else pltpu.roll(rows, 128 - 16 * b, 1)
            lat[b, at : at + rows.shape[0]] = value.astype(BF16)

    top, bot = rim_rows(place, rim)
    place_rows(0, top)
    for r in range(0, 16 * TILE, 64):
        place_rows(32 + r, recv[r : r + 64].astype(F32))
    place_rows(32 + 16 * TILE, bot)
    scale, offset = affine(stats, vectors[0:1], vectors[1:2], vectors[2:3])
    cell = lax.broadcasted_iota(jnp.int32, (16, CH), 0)
    hide_low = jnp.logical_and(cell == 0, place[1] == 0)
    hide_high = jnp.logical_and(cell == 15, place[1] == N_COL - 1)
    for i, value in enumerate((0.5 * scale, 0.5 * offset)):
        wide = jnp.broadcast_to(value, (16, CH))
        affines[i, 0] = jnp.where(hide_low, 0.0, wide)
        affines[i, 1] = wide
        affines[i, 2] = jnp.where(hide_high, 0.0, wide)
        affines[i, 3] = jnp.zeros((16, CH), F32)

    def contract(pair):
        patches = []
        for j in range(2):
            at = pl.multiple_of((2 * pair + j) * 16, 16)
            patches.append(
                jnp.concatenate(
                    [lat[b, pl.ds(at + 16 * a, 16)] for a in range(3) for b in range(3)], axis=0
                )
            )
        return dot_tn(jnp.concatenate(patches, axis=1), taps[...])

    def activate(pair, raw, pieces=range(4)):
        for j in range(2):
            row = 2 * pair + j
            hidden = jnp.logical_or(
                jnp.logical_and(row == 0, place[0] == 0),
                jnp.logical_and(row == ACT - 1, place[0] == N_ROW - 1),
            )
            for l in pieces:
                lanes = slice(128 * l, 128 * l + 128)
                for t in range(PLANES):
                    kind = jnp.where(hidden, 3, 0 if t == 0 else (2 if t == PLANES - 1 else 1))
                    at = 128 * j + 16 * t
                    half = raw[at : at + 16, lanes] * affines[0, kind, :, lanes]
                    half = half + affines[1, kind, :, lanes]
                    act[row, l, 16 * t : 16 * t + 16] = (half + half * jnp.tanh(half)).astype(BF16)

    def build(tile, slot, pieces=range(4)):
        base = pl.multiple_of((tile % BLOCK) * 32, 32)
        for l in pieces:
            rows = []
            for q in range(2):
                for t in range(len(rows), 4 + 2 * q):
                    d = [act[2 * tile + u, l, 16 * t : 16 * t + 16] for u in range(4)]
                    rows.append((d[0] - d[2], d[1] + d[2], d[2] - d[1], d[1] - d[3]))
                for u in range(4):
                    r = [rows[2 * q + v][u] for v in range(4)]
                    columns = (r[0] - r[2], r[1] + r[2], r[2] - r[1], r[1] - r[3])
                    for v in range(4):
                        slot[4 * u + v, l, pl.ds(base + 16 * q, 16)] = columns[v]

    def multiply(point, v_slot, m_slot, half):
        cells = jnp.concatenate([v_slot[point, l] for l in range(4)], axis=1)
        value = dot_nt(cells, points[point, 256 * half : 256 * half + 256])
        for i in range(2):
            m_slot[point, 2 * half + i] = value[:, 128 * i : 128 * i + 128]

    def finish(tile, slot, pieces=range(4)):
        base = pl.multiple_of((tile % BLOCK) * 32, 32)
        for l in pieces:
            bias = vectors[3:4, 128 * l : 128 * l + 128]
            for q in range(2):
                for h in range(2):
                    sums = []
                    for u in range(4):
                        m = [slot[4 * u + v, l, pl.ds(base + 16 * q + 8 * h, 8)] for v in range(4)]
                        if u == 1:
                            m[1] = m[1] + bias
                        both, apart = m[1] + m[2], m[1] - m[2]
                        sums.append((m[0] + both, apart - m[3]))
                    for f in range(2):
                        z = [sums[u][f] for u in range(4)]
                        both, apart = z[1] + z[2], z[1] - z[2]
                        at = pl.ds(32 * h + 2 * q + f, 8, stride=4)
                        spread[0, l, at] = z[0] + both
                        spread[1, l, at] = apart - z[3]
            for e in range(2):
                out[2 * tile + e, l] = spread[e, l].astype(BF16)

    for pair in range(2):
        activate(pair, contract(pair))

    def warm(c, _):
        value = contract(c + 2)
        build(c, v0)
        activate(c + 2, value)
        return 0

    lax.fori_loop(0, BLOCK, warm, 0)
    for load in loads:
        load.wait()
    last_pair = ACT // 2 - 1
    copies = []
    for n in range(N_BLOCK):
        this_v, next_v = v_slots[n % 2], v_slots[1 - n % 2]
        this_m, last_m = m_slots[n % 2], m_slots[1 - n % 2]

        def steady(c, _, n=n, this_v=this_v, next_v=next_v, this_m=this_m, last_m=last_m):
            first = n * BLOCK + c * TILES
            ahead = n < N_BLOCK - 1
            for k in range(TILES):
                g = first + k
                pair = jnp.minimum(g + BLOCK + 2, last_pair)
                if ahead:
                    value = contract(pair)
                for i in range(4):
                    multiply(2 * (c * TILES + k) + i // 2, this_v, this_m, i % 2)
                    if n > 0:
                        finish(g - BLOCK, last_m, (i,))
                    if ahead:
                        build(g + BLOCK, next_v, (i,))
                        activate(pair, value, (i,))
            return 0

        lax.fori_loop(0, BLOCK // TILES, steady, 0)
        if n > 0:
            copies.extend(send(out, out_hbm, n - 1, sems))

    def drain(c, _):
        finish((N_BLOCK - 1) * BLOCK + c, m_slots[1 - N_BLOCK % 2])
        return 0

    for half in range(2):
        lax.fori_loop(half * BLOCK // 2, (half + 1) * BLOCK // 2, drain, 0)
        copies.extend(send(out, out_hbm, N_BLOCK - 1 + half, sems, half))
    for copy in copies:
        copy.wait()


def send(out, out_hbm, n, sems, half=None):
    rows = slice(2 * BLOCK * n, 2 * BLOCK * (n + 1))
    if half is not None:
        first = 2 * BLOCK * (N_BLOCK - 1) + BLOCK * half
        rows = slice(first, first + BLOCK)
    copies = [
        pltpu.make_async_copy(
            out.at[rows, l], out_hbm.at[rows, :, 128 * l : 128 * l + 128], sems.at[n, l]
        )
        for l in range(4)
    ]
    for copy in copies:
        copy.start()
    return copies


def step(latent, in_weight, in_bias, norm_gain, norm_shift, mid_weight, mid_bias):
    both = ("row", "col")
    place = jnp.stack([lax.axis_index("row"), lax.axis_index("col")]).astype(jnp.int32)
    small = pltpu.CompilerParams(vmem_limit_bytes=12 * MIB)
    chunks = pl.pallas_call(
        pack_kernel,
        out_shape=jax.ShapeDtypeStruct((N_COL, 64, 128), BF16),
        in_specs=[VMEM],
        out_specs=VMEM,
        scratch_shapes=[pltpu.VMEM((64, WIDTH), BF16)],
        compiler_params=small,
        name="pack",
    )(latent)
    recv = lax.all_to_all(chunks, "col", split_axis=0, concat_axis=0, tiled=True)
    recv = recv.reshape(16 * TILE, 128)
    above = lax.broadcasted_iota(jnp.int32, (N_ROW, 32, 128), 0) > place[0]
    edges = jnp.where(above, recv[None, -32:], recv[None, :32])
    rim = lax.all_to_all(edges, "row", split_axis=0, concat_axis=0, tiled=True)
    sums, taps, vectors = pl.pallas_call(
        inner_kernel,
        out_shape=[
            jax.ShapeDtypeStruct((2, 8, CH), F32),
            jax.ShapeDtypeStruct((9 * C_LAT, CH), BF16),
            jax.ShapeDtypeStruct((4, CH), F32),
        ],
        in_specs=[VMEM] + [HBM] * 5,
        out_specs=[VMEM] * 3,
        scratch_shapes=[pltpu.VMEM((3, 16 * (TILE - 1), 128), BF16), pltpu.SemaphoreType.DMA((5,))],
        compiler_params=small,
        name="inner",
    )(
        recv,
        hbm(in_weight.reshape(9 * C_LAT, CH)),
        *(hbm(v.reshape(1, CH)) for v in (in_bias, norm_gain, norm_shift, mid_bias)),
    )
    partial = pl.pallas_call(
        outer_kernel,
        out_shape=jax.ShapeDtypeStruct((N_DEV, 1, 128), F32),
        in_specs=[SMEM] + [VMEM] * 5,
        out_specs=VMEM,
        compiler_params=small,
        name="outer",
    )(place, recv, rim, sums, taps, vectors)
    stats = lax.all_to_all(partial, both, split_axis=0, concat_axis=0, tiled=True)
    weight = hbm(jnp.transpose(mid_weight, (1, 2, 0, 3)))
    points = []
    for part in range(2):
        points.append(
            pl.pallas_call(
                prepare_kernel,
                out_shape=jax.ShapeDtypeStruct((16, CH // 2, CH), BF16),
                grid=(2,),
                in_specs=[
                    pl.BlockSpec((3, 3, CH // 4, CH), lambda i, part=part: (0, 0, i + 2 * part, 0))
                ],
                out_specs=pl.BlockSpec((16, CH // 4, CH), lambda i: (0, i, 0)),
                compiler_params=pltpu.CompilerParams(vmem_limit_bytes=60 * MIB),
            )(weight)
        )
    return pl.pallas_call(
        main_kernel,
        out_shape=jax.ShapeDtypeStruct((TILE, TILE, CH), BF16),
        in_specs=[SMEM] + [VMEM] * 5 + [HBM] * 2,
        out_specs=HBM,
        scratch_shapes=[
            pltpu.VMEM((3, LAT * 16, 128), BF16),
            pltpu.VMEM((ACT, 4, PLANES * 16, 128), BF16),
            pltpu.VMEM((2, 4, 16, CH), F32),
            pltpu.VMEM((256, CH), F32),
            pltpu.VMEM((16, 4, M_ROWS, 128), BF16),
            pltpu.VMEM((16, 4, M_ROWS, 128), BF16),
            pltpu.VMEM((16, 4, M_ROWS, 128), F32),
            pltpu.VMEM((16, 4, M_ROWS, 128), F32),
            pltpu.VMEM((2, 4, TILE, 128), F32),
            pltpu.VMEM((TILE, 4, TILE, 128), BF16),
            pltpu.VMEM((16, CH, CH), BF16),
            pltpu.SemaphoreType.DMA((2,)),
            pltpu.SemaphoreType.DMA((N_BLOCK + 1, 4)),
        ],
        compiler_params=pltpu.CompilerParams(vmem_limit_bytes=52 * MIB),
        name="main",
    )(
        place,
        recv,
        rim,
        stats,
        taps,
        vectors,
        hbm(points[0]),
        hbm(points[1]),
    )


def solution(mesh):
    in_specs = (P(None, ("row", "col")), P(), P(), P(), P(), P(), P())
    return jax.shard_map(
        step, mesh=mesh, in_specs=in_specs, out_specs=P("row", "col", None), check_vma=False
    )
```

```python
import functools

import jax
import jax.numpy as jnp
from jax import lax
from jax.experimental import pallas as pl
from jax.experimental.pallas import tpu as pltpu
from jax.sharding import PartitionSpec as P

C_LAT = 16
CH = 512
GROUPS = 32
TILE = 64
WIDTH = 1024
N_ROW = 8
N_COL = 16
N_DEV = N_ROW * N_COL
OWN = 4
ACT = TILE + 2
LAT = TILE + 4
PLANES = 6
EPSILON = 1e-06
BF16 = jnp.bfloat16
F32 = jnp.float32
VMEM = pl.BlockSpec(memory_space=pltpu.VMEM)
SMEM = pl.BlockSpec(memory_space=pltpu.SMEM)
HBM = pl.BlockSpec(memory_space=pltpu.HBM)
MIB = 1 << 20


def dot_tn(lhs, rhs):
    return lax.dot_general(lhs, rhs, (((0,), (0,)), ((), ())), preferred_element_type=F32)


def dot_nt(lhs, rhs):
    return lax.dot_general(lhs, rhs, (((1,), (1,)), ((), ())), preferred_element_type=F32)


def hbm(array):
    return pltpu.with_memory_space_constraint(array, pltpu.HBM)


def start_copies(sources, targets, sems):
    copies = [
        pltpu.make_async_copy(source, target, sems.at[i])
        for i, (source, target) in enumerate(zip(sources, targets))
    ]
    for copy in copies:
        copy.start()
    return copies


def pack_kernel(own, out, rows):
    k = lax.broadcasted_iota(jnp.int32, (384, 256), 0)
    n = lax.broadcasted_iota(jnp.int32, (384, 256), 1)
    lane = n % 128
    column = 64 * (n // 128) + 4 * (lane % 16) + lane // 16 + 126
    pick = jnp.where(k == column, 1.0, 0.0).astype(BF16)
    zero = jnp.zeros((64, 128), BF16)
    for r in range(OWN):
        rows[16 * r : 16 * r + 16] = own[:, WIDTH * r : WIDTH * (r + 1)]
    for t in range(8):
        parts = [
            rows[:, 128 * u : 128 * (u + 1)] if 0 <= u < 8 else zero for u in (t - 1, t, t + 1)
        ]
        moved = jnp.dot(jnp.concatenate(parts, axis=1), pick, preferred_element_type=F32)
        out[2 * t] = moved[:, :128].astype(BF16)
        out[2 * t + 1] = moved[:, 128:].astype(BF16)


def add_cells(value, total, squares):
    value = value.reshape(value.shape[0] // 8, 8, CH)
    return total + jnp.sum(value, axis=0), squares + jnp.sum(value * value, axis=0)


def inner_kernel(
    recv, weight_hbm, bias_hbm, gain_hbm, shift_hbm, mid_bias_hbm, sums, weight, vectors, pairs, sems
):
    copies = start_copies(
        (weight_hbm, bias_hbm, gain_hbm, shift_hbm, mid_bias_hbm),
        (weight, *(vectors.at[i : i + 1] for i in range(4))),
        sems,
    )
    rows = recv[...].astype(F32)
    low = lax.broadcasted_iota(jnp.int32, (16 * (TILE - 1), 128), 1) < 64
    for b in range(3):
        even = pltpu.roll(rows, 112 - 16 * b, 1)
        odd = pltpu.roll(rows, (176 - 16 * b) % 128, 1)
        pairs[b] = jnp.where(low, even[:-16], odd[16:]).astype(BF16)
    for copy in copies:
        copy.wait()

    def contract(first, count):
        patches = [
            jnp.concatenate(
                [
                    pairs[b, pl.ds(pl.multiple_of((2 * (first + j) + a) * 16, 16), 16)]
                    for a in range(3)
                    for b in range(3)
                ],
                axis=0,
            )
            for j in range(count)
        ]
        return dot_tn(jnp.concatenate(patches, axis=1), weight[...])

    def accumulate(i, carry):
        values = [contract(GANG * i + 4 * part, 4) for part in range(GANG // 4)]
        for value in values:
            carry = add_cells(value, *carry)
        return carry

    zero = jnp.zeros((8, CH), F32)
    whole = 28 // GANG
    carry = lax.fori_loop(0, whole, accumulate, (zero, zero))
    sums[0], sums[1] = add_cells(contract(28, 3), *carry)


GANG = 28


def rim_rows(place, rim):
    top = rim[jnp.maximum(place[0] - 1, 0)].astype(F32)
    bot = rim[jnp.minimum(place[0] + 1, N_ROW - 1)].astype(F32)
    top = jnp.where(place[0] == 0, 0.0, top)
    return top, jnp.where(place[0] == N_ROW - 1, 0.0, bot)


def outer_kernel(place, recv, rim, sums, weight, vectors, out):
    channel = lax.broadcasted_iota(jnp.int32, (CH, 128), 0) // (CH // GROUPS)
    lane = lax.broadcasted_iota(jnp.int32, (CH, 128), 1)
    to_sum = jnp.where(channel == lane, 1.0, 0.0)
    top, bot = rim_rows(place, rim)
    first = jnp.concatenate([top[16:], recv[0:32].astype(F32)], axis=0)
    last = jnp.concatenate([recv[16 * TILE - 32 :].astype(F32), bot[:16]], axis=0)
    low = lax.broadcasted_iota(jnp.int32, (48, 128), 1) < 64
    shifted = [
        jnp.where(
            low, pltpu.roll(first, 112 - 16 * b, 1), pltpu.roll(last, (176 - 16 * b) % 128, 1)
        ).astype(BF16)
        for b in range(3)
    ]
    patch = jnp.concatenate(
        [shifted[b][16 * a : 16 * a + 16] for a in range(3) for b in range(3)], axis=0
    )
    total, squares = add_cells(dot_tn(patch, weight[...]), sums[0], sums[1])
    bias = vectors[0:1]
    cells = TILE * TILE // 8
    squares = squares + bias * (2.0 * total + cells * bias)
    total = total + cells * bias
    exact = functools.partial(
        jnp.dot, precision=lax.Precision.HIGHEST, preferred_element_type=F32
    )
    both = exact(jnp.concatenate([total, squares], axis=0), to_sum)
    both = both[0:8] + pltpu.roll(both[8:16], GROUPS, 1)
    out[...] = jnp.broadcast_to(jnp.sum(both, axis=0).reshape(1, 1, 128), (N_DEV, 1, 128))


def affine(stats, bias, gain, shift):
    sums = jnp.sum(stats[...], axis=0)
    sums = jnp.broadcast_to(sums, (8, 128)) / (TILE * TILE * N_DEV * (CH // GROUPS))
    channel = lax.broadcasted_iota(jnp.int32, (128, CH), 1) // (CH // GROUPS)
    lane = lax.broadcasted_iota(jnp.int32, (128, CH), 0)
    spread = functools.partial(
        jnp.dot, precision=lax.Precision.HIGHEST, preferred_element_type=F32
    )
    rows = jnp.concatenate([sums, pltpu.roll(sums, 128 - GROUPS, 1)], axis=0)
    moments = spread(rows, jnp.where(channel == lane, 1.0, 0.0))
    mean, square = moments[0:1], moments[8:9]
    scale = lax.rsqrt(square - mean * mean + EPSILON) * gain[...]
    return scale, (bias[...] - mean) * scale + shift[...]


def prepare_kernel(weight, points):
    def thirds(g):
        even = 0.5 * (g[0] + g[2])
        odd = 0.5 * g[1]
        return g[0], even + odd, even - odd, g[2]

    def transform(step, _):
        rows = pl.ds(pl.multiple_of(step * 16, 16), 16)
        for l in range(4):
            lanes = slice(128 * l, 128 * l + 128)
            columns = [
                thirds([weight[a, b, rows, lanes].astype(F32) for a in range(3)]) for b in range(3)
            ]
            for u in range(4):
                for v, value in enumerate(thirds([columns[b][u] for b in range(3)])):
                    points[4 * u + v, rows, lanes] = value.astype(BF16)
        return 0

    lax.fori_loop(0, weight.shape[2] // 16, transform, 0)


BLOCK = 8
TILES = 4
N_BLOCK = TILE // 2 // BLOCK
M_ROWS = BLOCK * 32


def main_kernel(
    place,
    recv,
    rim,
    stats,
    taps,
    vectors,
    low_hbm,
    high_hbm,
    out_hbm,
    lat,
    act,
    affines,
    raw,
    v0,
    v1,
    m0,
    m1,
    spread,
    out,
    points,
    in_sems,
    sems,
):
    loads = start_copies(
        (low_hbm, high_hbm), (points.at[:, : CH // 2], points.at[:, CH // 2 :]), in_sems
    )

    v_slots, m_slots = (v0, v1), (m0, m1)

    def place_rows(at, rows):
        for b in range(3):
            value = rows if b == 0 else pltpu.roll(rows, 128 - 16 * b, 1)
            lat[b, at : at + rows.shape[0]] = value.astype(BF16)

    top, bot = rim_rows(place, rim)
    place_rows(0, top)
    for r in range(0, 16 * TILE, 64):
        place_rows(32 + r, recv[r : r + 64].astype(F32))
    place_rows(32 + 16 * TILE, bot)
    scale, offset = affine(stats, vectors[0:1], vectors[1:2], vectors[2:3])
    cell = lax.broadcasted_iota(jnp.int32, (16, CH), 0)
    hide_low = jnp.logical_and(cell == 0, place[1] == 0)
    hide_high = jnp.logical_and(cell == 15, place[1] == N_COL - 1)
    for i, value in enumerate((0.5 * scale, 0.5 * offset)):
        wide = jnp.broadcast_to(value, (16, CH))
        affines[i, 0] = jnp.where(hide_low, 0.0, wide)
        affines[i, 1] = wide
        affines[i, 2] = jnp.where(hide_high, 0.0, wide)
        affines[i, 3] = jnp.zeros((16, CH), F32)

    def contract(pair):
        patches = []
        for j in range(2):
            at = pl.multiple_of((2 * pair + j) * 16, 16)
            patches.append(
                jnp.concatenate(
                    [lat[b, pl.ds(at + 16 * a, 16)] for a in range(3) for b in range(3)], axis=0
                )
            )
        return dot_tn(jnp.concatenate(patches, axis=1), taps[...])

    def activate(pair, raw, pieces=range(4)):
        for j in range(2):
            row = 2 * pair + j
            hidden = jnp.logical_or(
                jnp.logical_and(row == 0, place[0] == 0),
                jnp.logical_and(row == ACT - 1, place[0] == N_ROW - 1),
            )
            for l in pieces:
                lanes = slice(128 * l, 128 * l + 128)
                for t in range(PLANES):
                    kind = jnp.where(hidden, 3, 0 if t == 0 else (2 if t == PLANES - 1 else 1))
                    at = 128 * j + 16 * t
                    half = raw[at : at + 16, lanes] * affines[0, kind, :, lanes]
                    half = half + affines[1, kind, :, lanes]
                    act[row, l, 16 * t : 16 * t + 16] = (half + half * jnp.tanh(half)).astype(BF16)

    def build(tile, slot, pieces=range(4)):
        base = pl.multiple_of((tile % BLOCK) * 32, 32)
        for l in pieces:
            rows = []
            for q in range(2):
                for t in range(len(rows), 4 + 2 * q):
                    d = [act[2 * tile + u, l, 16 * t : 16 * t + 16] for u in range(4)]
                    rows.append((d[0] - d[2], d[1] + d[2], d[2] - d[1], d[1] - d[3]))
                for u in range(4):
                    r = [rows[2 * q + v][u] for v in range(4)]
                    columns = (r[0] - r[2], r[1] + r[2], r[2] - r[1], r[1] - r[3])
                    for v in range(4):
                        slot[4 * u + v, l, pl.ds(base + 16 * q, 16)] = columns[v]

    def multiply(point, v_slot, m_slot, half):
        cells = jnp.concatenate([v_slot[point, l] for l in range(4)], axis=1)
        value = dot_nt(cells, points[point, 256 * half : 256 * half + 256])
        for i in range(2):
            m_slot[point, 2 * half + i] = value[:, 128 * i : 128 * i + 128]

    def finish(tile, slot, pieces=range(4)):
        base = pl.multiple_of((tile % BLOCK) * 32, 32)
        for l in pieces:
            bias = vectors[3:4, 128 * l : 128 * l + 128]
            for q in range(2):
                for h in range(2):
                    sums = []
                    for u in range(4):
                        m = [slot[4 * u + v, l, pl.ds(base + 16 * q + 8 * h, 8)] for v in range(4)]
                        both, apart = m[1] + m[2], m[1] - m[2]
                        sums.append((m[0] + both, apart - m[3]))
                    for f in range(2):
                        z = [sums[u][f] for u in range(4)]
                        both, apart = z[1] + z[2], z[1] - z[2]
                        at = pl.ds(32 * h + 2 * q + f, 8, stride=4)
                        spread[0, l, at] = z[0] + both + bias
                        spread[1, l, at] = apart - z[3] + bias
            for e in range(2):
                out[2 * tile + e, l] = spread[e, l].astype(BF16)

    for pair in range(2):
        activate(pair, contract(pair))

    def warm(c, _):
        value = contract(c + 2)
        build(c, v0)
        activate(c + 2, value)
        return 0

    lax.fori_loop(0, BLOCK, warm, 0)
    for load in loads:
        load.wait()
    last_pair = ACT // 2 - 1
    copies = []
    for n in range(N_BLOCK):
        this_v, next_v = v_slots[n % 2], v_slots[1 - n % 2]
        this_m, last_m = m_slots[n % 2], m_slots[1 - n % 2]

        def steady(c, _, n=n, this_v=this_v, next_v=next_v, this_m=this_m, last_m=last_m):
            first = n * BLOCK + c * TILES
            ahead = n < N_BLOCK - 1
            for k in range(TILES):
                g = first + k
                pair = jnp.minimum(g + BLOCK + 2, last_pair)
                if ahead:
                    value = contract(pair)
                for i in range(4):
                    multiply(2 * (c * TILES + k) + i // 2, this_v, this_m, i % 2)
                    if n > 0:
                        finish(g - BLOCK, last_m, (i,))
                    if ahead:
                        build(g + BLOCK, next_v, (i,))
                        activate(pair, value, (i,))
            return 0

        lax.fori_loop(0, BLOCK // TILES, steady, 0)
        if n > 0:
            copies.extend(send(out, out_hbm, n - 1, sems))

    def drain(c, _):
        finish((N_BLOCK - 1) * BLOCK + c, m_slots[1 - N_BLOCK % 2])
        return 0

    for half in range(2):
        lax.fori_loop(half * BLOCK // 2, (half + 1) * BLOCK // 2, drain, 0)
        copies.extend(send(out, out_hbm, N_BLOCK - 1 + half, sems, half))
    for copy in copies:
        copy.wait()


def send(out, out_hbm, n, sems, half=None):
    rows = slice(2 * BLOCK * n, 2 * BLOCK * (n + 1))
    if half is not None:
        first = 2 * BLOCK * (N_BLOCK - 1) + BLOCK * half
        rows = slice(first, first + BLOCK)
    copies = [
        pltpu.make_async_copy(
            out.at[rows, l], out_hbm.at[rows, :, 128 * l : 128 * l + 128], sems.at[n, l]
        )
        for l in range(4)
    ]
    for copy in copies:
        copy.start()
    return copies


def step(latent, in_weight, in_bias, norm_gain, norm_shift, mid_weight, mid_bias):
    both = ("row", "col")
    place = jnp.stack([lax.axis_index("row"), lax.axis_index("col")]).astype(jnp.int32)
    small = pltpu.CompilerParams(vmem_limit_bytes=12 * MIB)
    chunks = pl.pallas_call(
        pack_kernel,
        out_shape=jax.ShapeDtypeStruct((N_COL, 64, 128), BF16),
        in_specs=[VMEM],
        out_specs=VMEM,
        scratch_shapes=[pltpu.VMEM((64, WIDTH), BF16)],
        compiler_params=small,
        name="pack",
    )(latent)
    recv = lax.all_to_all(chunks, "col", split_axis=0, concat_axis=0, tiled=True)
    recv = recv.reshape(16 * TILE, 128)
    above = lax.broadcasted_iota(jnp.int32, (N_ROW, 32, 128), 0) > place[0]
    edges = jnp.where(above, recv[None, -32:], recv[None, :32])
    rim = lax.all_to_all(edges, "row", split_axis=0, concat_axis=0, tiled=True)
    sums, taps, vectors = pl.pallas_call(
        inner_kernel,
        out_shape=[
            jax.ShapeDtypeStruct((2, 8, CH), F32),
            jax.ShapeDtypeStruct((9 * C_LAT, CH), BF16),
            jax.ShapeDtypeStruct((4, CH), F32),
        ],
        in_specs=[VMEM] + [HBM] * 5,
        out_specs=[VMEM] * 3,
        scratch_shapes=[pltpu.VMEM((3, 16 * (TILE - 1), 128), BF16), pltpu.SemaphoreType.DMA((5,))],
        compiler_params=small,
        name="inner",
    )(
        recv,
        hbm(in_weight.reshape(9 * C_LAT, CH)),
        *(hbm(v.reshape(1, CH)) for v in (in_bias, norm_gain, norm_shift, mid_bias)),
    )
    partial = pl.pallas_call(
        outer_kernel,
        out_shape=jax.ShapeDtypeStruct((N_DEV, 1, 128), F32),
        in_specs=[SMEM] + [VMEM] * 5,
        out_specs=VMEM,
        compiler_params=small,
        name="outer",
    )(place, recv, rim, sums, taps, vectors)
    stats = lax.all_to_all(partial, both, split_axis=0, concat_axis=0, tiled=True)
    weight = hbm(jnp.transpose(mid_weight, (1, 2, 0, 3)))
    points = []
    for part in range(2):
        points.append(
            pl.pallas_call(
                prepare_kernel,
                out_shape=jax.ShapeDtypeStruct((16, CH // 2, CH), BF16),
                grid=(2,),
                in_specs=[
                    pl.BlockSpec((3, 3, CH // 4, CH), lambda i, part=part: (0, 0, i + 2 * part, 0))
                ],
                out_specs=pl.BlockSpec((16, CH // 4, CH), lambda i: (0, i, 0)),
                compiler_params=pltpu.CompilerParams(vmem_limit_bytes=60 * MIB),
            )(weight)
        )
    return pl.pallas_call(
        main_kernel,
        out_shape=jax.ShapeDtypeStruct((TILE, TILE, CH), BF16),
        in_specs=[SMEM] + [VMEM] * 5 + [HBM] * 2,
        out_specs=HBM,
        scratch_shapes=[
            pltpu.VMEM((3, LAT * 16, 128), BF16),
            pltpu.VMEM((ACT, 4, PLANES * 16, 128), BF16),
            pltpu.VMEM((2, 4, 16, CH), F32),
            pltpu.VMEM((256, CH), F32),
            pltpu.VMEM((16, 4, M_ROWS, 128), BF16),
            pltpu.VMEM((16, 4, M_ROWS, 128), BF16),
            pltpu.VMEM((16, 4, M_ROWS, 128), F32),
            pltpu.VMEM((16, 4, M_ROWS, 128), F32),
            pltpu.VMEM((2, 4, TILE, 128), F32),
            pltpu.VMEM((TILE, 4, TILE, 128), BF16),
            pltpu.VMEM((16, CH, CH), BF16),
            pltpu.SemaphoreType.DMA((2,)),
            pltpu.SemaphoreType.DMA((N_BLOCK + 1, 4)),
        ],
        compiler_params=pltpu.CompilerParams(vmem_limit_bytes=52 * MIB),
        name="main",
    )(
        place,
        recv,
        rim,
        stats,
        taps,
        vectors,
        hbm(points[0]),
        hbm(points[1]),
    )


def solution(mesh):
    in_specs = (P(None, ("row", "col")), P(), P(), P(), P(), P(), P())
    return jax.shard_map(
        step, mesh=mesh, in_specs=in_specs, out_specs=P("row", "col", None), check_vma=False
    )
```
